32 devices in a mesh: groups: 2 (over y), sec: 4 (over z), strip: 4 (over x, core).
Axes of the slice: x: 2, y: 2, z: 4, core: 2. Of those that a mesh axis runs over, the one named last changes fastest.
Arguments:
- sections: bfloat16 [4, 256, 1024], P('sec', 'strip', 'groups'), parts along dimension 2, may hold values from -40 to 40
- mask_fine: int32 [4, 8, 32], P('sec', 'strip', 'groups'), parts along dimension 2, may hold values 0 or 1
- mask_coarse: int32 [4, 4, 16], P('sec', 'strip', 'groups'), parts along dimension 2, may hold values 0 or 1
Outputs:
- corr_fine: float32 [4, 2, 8, 32, 1024], P('sec', None, 'strip', 'groups'), parts along dimension 3
- corr_coarse: float32 [4, 2, 4, 16, 1024], P('sec', None, 'strip', 'groups'), parts along dimension 3
The draws below stay inside these ranges and needn't reach their ends.
There are 2 independent parts, one for each index of `groups`. The reference program is written for one: setup_inputs(seed, part) draws one part's arguments, and reference() takes and returns one part's arrays. A program takes and returns all parts, laid end to end along the dimension named above; each array names one. Nothing has to cross between parts.
All inputs are finite; a program needn't handle non-finite values. No bound on the sum of `mask_fine` or of `mask_coarse` on one device may be relied on, other than what follows from the above.
Results may differ from the reference program's by a relative error of at most 0.0039.
Values may be sent and summed in bfloat16 or wider, within the bound.
A program may use at most 64 MiB of HBM per device.

```python
import jax
import jax.numpy as jnp
from jax import lax

PATCH = 64
STRIDE = 32
WINDOW = 32
WIDTH = 512
NZ = 4
H = 256


def draw_sections(key, part):
    key_noise, key_rows, key_cols = jax.random.split(key, 3)
    row_scale = jnp.exp(jax.random.uniform(key_rows, (NZ, H, 1), jnp.float32, 0.0, jnp.log(10.0)))
    col_scale = jnp.exp(jax.random.uniform(key_cols, (NZ, 1, WIDTH), jnp.float32, 0.0, jnp.log(10.0)))
    scaling = jnp.sqrt(row_scale * col_scale)
    section_image = jax.random.normal(key_noise, (NZ, H, WIDTH), jnp.float32) * scaling
    return jnp.clip(section_image, -40.0, 40.0).astype(jnp.bfloat16)


def set_ends(drawn, rng, low, top_value):
    index_at = [jax.random.randint(jax.random.fold_in(rng, axis), (), 0, length) for axis, length in enumerate(drawn.shape)]
    main_axis = drawn.shape.index(max(drawn.shape))
    beside = index_at[:main_axis] + [(index_at[main_axis] + 1) % drawn.shape[main_axis]] + index_at[main_axis + 1:]
    return drawn.at[tuple(index_at)].set(low).at[tuple(beside)].set(top_value)


def setup_inputs(seed: int = 0, part: int = 0) -> dict:
    splits = jax.random.split(jax.random.key(seed), 4)
    part_keys = jax.random.split(jax.random.fold_in(splits[3], part), 4)
    return {
        "sections": draw_sections(jax.random.fold_in(jax.random.fold_in(splits[3], part), 71), part),
        "mask_fine": set_ends((jax.random.randint(part_keys[1], (NZ, H // STRIDE, WIDTH // STRIDE), 0, 4) < 3).astype(jnp.int32), jax.random.fold_in(part_keys[1], 1), 0, 1),
        "mask_coarse": set_ends((jax.random.randint(part_keys[2], (NZ, H // (2 * STRIDE), WIDTH // (2 * STRIDE)), 0, 4) < 3).astype(jnp.int32), jax.random.fold_in(part_keys[2], 1), 0, 1),
    }


def make_patches(section_image, patch_rows, patch_cols):
    blocks = section_image.reshape(patch_rows + 1, STRIDE, patch_cols + 1, STRIDE)
    tall_blocks = jnp.concatenate([blocks[:-1], blocks[1:]], axis=1)
    wide_blocks = jnp.concatenate([tall_blocks[:, :, :-1], tall_blocks[:, :, 1:]], axis=3)
    return wide_blocks.transpose(1, 3, 0, 2).reshape(PATCH, PATCH, patch_rows * patch_cols)

def level_patches(extended):
    strip_rows = extended.shape[0] - PATCH
    section_width = extended.shape[1]
    fine_img = jnp.pad(extended[:strip_rows + STRIDE], ((0, 0), (0, STRIDE)))
    pooled = extended.reshape(extended.shape[0] // 2, 2, section_width // 2, 2).mean(axis=(1, 3))
    coarse_img = jnp.pad(pooled, ((0, 0), (0, STRIDE)))
    fine_patches = make_patches(fine_img, strip_rows // STRIDE, section_width // STRIDE)
    coarse_patches = make_patches(coarse_img, strip_rows // (2 * STRIDE), section_width // (2 * STRIDE))
    return jnp.concatenate([fine_patches, coarse_patches], axis=2)

def section_spectra(section_image):
    extended = jnp.pad(section_image.astype(jnp.float32), ((0, PATCH), (0, 0)))
    patches = level_patches(extended)
    centered = patches - lax.optimization_barrier(jnp.mean(patches, axis=(0, 1)))
    unit_patch = centered / jnp.sqrt(lax.optimization_barrier(jnp.mean(centered * centered, axis=(0, 1))) + 1e-05)
    spectrum = jnp.fft.fft2(unit_patch, axes=(0, 1))
    return jnp.stack([spectrum.real, spectrum.imag]).astype(jnp.bfloat16)

def window_correlation(own_spec, other_spec):
    own_spec = own_spec.astype(jnp.float32)
    other_spec = other_spec.astype(jnp.float32)
    cross_real = own_spec[0] * other_spec[0] + own_spec[1] * other_spec[1]
    cross_imag = own_spec[0] * other_spec[1] - own_spec[1] * other_spec[0]
    cross_spec = cross_real + 1j * cross_imag
    full_map = jnp.fft.ifft2(cross_spec, axes=(0, 1)).real
    shift_index = ((jnp.arange(WINDOW) - WINDOW // 2) % PATCH).astype(jnp.int32)
    picked = jnp.take(jnp.take(full_map, shift_index, axis=0), shift_index, axis=1)
    return picked / PATCH

def reference(sections, mask_fine, mask_coarse):
    spectra_all = lax.map(section_spectra, sections)
    zero_sections = jnp.zeros((2,) + spectra_all.shape[1:], spectra_all.dtype)
    padded = jnp.concatenate([spectra_all, zero_sections], axis=0)
    fine_rows = H // STRIDE
    fine_cols = WIDTH // STRIDE
    coarse_rows = H // (2 * STRIDE)
    coarse_cols = WIDTH // (2 * STRIDE)
    fine_count = fine_rows * fine_cols

    def one_section(section_items):
        own_spec, first_spec, second_spec, fine_mask, coarse_mask = section_items
        corr_maps = jnp.stack([window_correlation(own_spec, first_spec), window_correlation(own_spec, second_spec)])
        flat_maps = corr_maps.reshape(2, WINDOW * WINDOW, -1)
        fine_out = flat_maps[:, :, :fine_count].reshape(2, WINDOW * WINDOW, fine_rows, fine_cols).transpose(0, 2, 3, 1)
        coarse_out = flat_maps[:, :, fine_count:].reshape(2, WINDOW * WINDOW, coarse_rows, coarse_cols).transpose(0, 2, 3, 1)
        fine_out = fine_out * fine_mask.astype(jnp.float32)[None, :, :, None]
        coarse_out = coarse_out * coarse_mask.astype(jnp.float32)[None, :, :, None]
        return (fine_out, coarse_out)
    corr_fine, corr_coarse = lax.map(one_section, (padded[:NZ], padded[1:NZ + 1], padded[2:NZ + 2], mask_fine, mask_coarse))
    return (corr_fine, corr_coarse)
```

```python
import functools

import jax
import jax.numpy as jnp
import numpy as np
from jax import lax
from jax.experimental import pallas as pl
from jax.experimental.pallas import tpu as pltpu
from jax.sharding import PartitionSpec as P

PATCH = 64
STRIDE = 32
WINDOW = 32
HALF = PATCH // 2 + 1
KP = 40
CHUNKS = 2
GRANT = 48 * 1024 * 1024
LANES = 128
F32 = jnp.float32
BF16 = jnp.bfloat16
MESH = pl.DeviceIdType.MESH


def trig(phase):
    angle = 2.0 * np.pi / PATCH * np.mod(phase, PATCH)
    return np.round(np.cos(angle), 12), np.round(np.sin(angle), 12)


def split(table):
    high = np.asarray(table, np.float32).astype(BF16)
    low = (np.asarray(table, np.float64) - high.astype(np.float64)).astype(np.float32).astype(BF16)
    return high, low


def block_diagonal(block, count):
    return np.kron(np.eye(count), block)


def tables(strip_rows):
    fine_rows = strip_rows // STRIDE
    coarse_rows = strip_rows // (2 * STRIDE)
    height = strip_rows + PATCH
    k = np.arange(KP)[:, None]
    keep = (k < HALF).astype(np.float64)
    x = np.arange(height)[None, :]
    units = []
    for i in range(fine_rows):
        c, s = trig(k * (x - STRIDE * i))
        inside = ((x >= STRIDE * i) & (x < STRIDE * i + PATCH)) * keep
        units += [c * inside, -s * inside]
    for i in range(coarse_rows):
        xc = x // 2 - STRIDE * i
        c, s = trig(k * xc)
        inside = ((xc >= 0) & (xc < PATCH)) * keep * 0.25
        units += [c * inside, -s * inside]
    a_high, a_low = split(np.concatenate(units, axis=0))
    first = np.concatenate([a_high, a_low], axis=1)

    freq = np.arange(PATCH)[None, :]
    y = np.arange(STRIDE)[:, None]
    c, s = trig(y * freq)

    def second(c, s, count):
        c, s = block_diagonal(c, count), block_diagonal(s, count)
        return split(np.block([[c, -s], [s, c]]))

    fine_w = second(c, s, LANES // STRIDE)
    coarse_w = second(np.repeat(c, 2, axis=0), np.repeat(s, 2, axis=0), LANES // (2 * STRIDE))

    shift = np.arange(WINDOW) - WINDOW // 2
    c, s = trig(np.arange(PATCH)[:, None] * shift[None, :])
    c, s = block_diagonal(c, 4), block_diagonal(s, 4)
    inverse = split(np.block([[c, s], [-s, c]]))

    weight = np.where((k == 0) | (k == PATCH // 2), 1.0, 2.0) * keep
    c, s = trig(shift[:, None] * np.arange(KP)[None, :])
    last_high, last_low = split(np.concatenate([c * weight.T, -s * weight.T], axis=1))
    last = np.concatenate([last_high, last_high, last_low], axis=1)
    energy = np.kron(np.eye(4), np.ones((PATCH, WINDOW)))
    return [
        first,
        *fine_w,
        *coarse_w,
        *inverse,
        last,
        np.asarray(energy, np.float32),
        np.asarray(np.broadcast_to(weight, (KP, LANES)), np.float32),
    ]


def split_value(value):
    high = value.astype(BF16)
    return high, (value - high.astype(F32)).astype(BF16)


def matmul(a, b):
    return jnp.dot(a, b, preferred_element_type=F32)


def section_spectra(pixels, first, fine_w, coarse_w, fine_rows, coarse_rows):
    half = matmul(first, jnp.concatenate([pixels, pixels], axis=0))
    width = half.shape[1]
    tiles = width // LANES
    row = lax.broadcasted_iota(jnp.int32, (KP, width), 0)
    fine_in, coarse_in = [], []
    for unit in range(fine_rows + coarse_rows):
        real = half[2 * KP * unit : 2 * KP * unit + KP]
        imag = half[2 * KP * unit + KP : 2 * KP * (unit + 1)]
        sums = real[0:1]
        high = sums.astype(BF16).astype(F32)
        middle = (sums - high).astype(BF16).astype(F32)
        low = sums - high - middle
        real = jnp.where(row == 0, high, real)
        real = jnp.where(row == HALF, middle, real)
        real = jnp.where(row == HALF + 1, low, real)
        target = fine_in if unit < fine_rows else coarse_in
        for tile in range(tiles):
            at = slice(LANES * tile, LANES * (tile + 1))
            target.append(jnp.concatenate([real[:, at], imag[:, at]], axis=1))

    def transform(parts, weights):
        high, low = split_value(jnp.concatenate(parts, axis=0))
        w_high, w_low = weights
        return matmul(high, w_high) + matmul(low, w_high) + matmul(high, w_low)

    fine = transform(fine_in, fine_w)
    coarse = transform(coarse_in, coarse_w)
    wide = 2 * LANES
    lane = lax.broadcasted_iota(jnp.int32, (KP, wide), 1)
    krow = lax.broadcasted_iota(jnp.int32, (KP, wide), 0)
    sign = jnp.where(lane % 2 == 0, 1.0, -1.0).astype(F32)
    dc = (krow == 0) & (lane % PATCH == 0)

    def finish(parts, rows):
        count = len(parts) // rows
        rolled = [pltpu.roll(part, wide - PATCH, 1) for part in parts]
        done = []
        for index, part in enumerate(parts):
            if index % count == count - 1:
                following = jnp.where(lane < wide - PATCH, rolled[index], 0.0)
            else:
                following = jnp.where(lane < wide - PATCH, rolled[index], rolled[index + 1])
            value = part + sign * following
            value = jnp.where(krow == 0, value + value[HALF : HALF + 1] + value[HALF + 1 : HALF + 2], value)
            value = jnp.where(dc, 0.0, value)
            done.append(value)
        return done

    def groups(offset):
        fine_parts = [
            fine[KP * g : KP * (g + 1), offset * wide : (offset + 1) * wide]
            for g in range(fine_rows * tiles)
        ]
        coarse_parts = [
            jnp.concatenate(
                [
                    coarse[KP * g : KP * (g + 1), offset * LANES : (offset + 1) * LANES],
                    coarse[KP * (g + 1) : KP * (g + 2), offset * LANES : (offset + 1) * LANES],
                ],
                axis=1,
            )
            for g in range(0, coarse_rows * tiles, 2)
        ]
        return finish(fine_parts, fine_rows) + finish(coarse_parts, coarse_rows)

    return groups(0), groups(1)


def block_transpose(value):
    row = lax.broadcasted_iota(jnp.int32, value.shape, 0) % 4
    block = lax.broadcasted_iota(jnp.int32, value.shape, 1) // WINDOW
    rows = value.shape[0]
    moved = pltpu.roll(value, 2 * WINDOW, 1)
    other = jnp.where(row < 2, pltpu.roll(moved, rows - 2, 0), pltpu.roll(moved, 2, 0))
    value = jnp.where((row // 2) == (block // 2), value, other)
    right = pltpu.roll(pltpu.roll(value, WINDOW, 1), rows - 1, 0)
    left = pltpu.roll(pltpu.roll(value, LANES - WINDOW, 1), 1, 0)
    other = jnp.where(row % 2 == 0, right, left)
    return jnp.where((row % 2) == (block % 2), value, other)


def compute(const_count, *refs):
    pixels_ref, fine_mask_ref, coarse_mask_ref = refs[:3]
    sources = refs[3 : 3 + const_count]
    fine_out_ref, coarse_out_ref = refs[3 + const_count : 5 + const_count]
    main_ref, rim_ref, real_ref, imag_ref, sums_ref, scale_ref = refs[5 + const_count : 11 + const_count]
    held = refs[11 + const_count : 11 + 2 * const_count]
    own_sem, const_sem, send_sem, main_sem, rim_sem = refs[11 + 2 * const_count :]
    sec, strip = lax.axis_index("sec"), lax.axis_index("strip")
    secs, strips = lax.axis_size("sec"), lax.axis_size("strip")
    even, odd = strip % 2 == 0, strip % 2 == 1
    below = strip + 1 < strips
    has_near, has_far = sec + 1 < secs, sec + 2 < secs

    barrier = pltpu.get_barrier_semaphore()

    def greet(condition, device):
        @pl.when(condition)
        def _():
            pl.semaphore_signal(barrier, inc=1, device_id=device, device_id_type=MESH)

    greet(even & has_far, {"sec": sec + 2})
    greet(odd & has_near & below, {"sec": sec + 1, "strip": strip + 1})
    greet(has_near, {"sec": sec + 1})
    greet(below, {"strip": strip + 1})

    own_copy = pltpu.make_async_copy(pixels_ref.at[0], main_ref.at[0], own_sem)
    own_copy.start()
    const_copies = [
        pltpu.make_async_copy(source, target, const_sem.at[index])
        for index, (source, target) in enumerate(zip(sources, held))
    ]
    for copy in const_copies:
        copy.start()

    diagonal = even & (sec >= 1) & (strip >= 1)
    routed = even & (sec >= 2)
    one = lambda condition: jnp.where(condition, 1, 0)
    targets = one(sec >= 1) + one(strip >= 1) + one(diagonal) + one(routed)

    @pl.when(targets >= 1)
    def _():
        pl.semaphore_wait(barrier, targets)

    piece = pixels_ref.shape[2] // CHUNKS

    def remote(flow, source, target, sems, section, device):
        def chunk(c):
            columns = (slice(None), pl.ds(piece * c, piece))
            return pltpu.make_async_remote_copy(
                src_ref=source.at[columns],
                dst_ref=target.at[section].at[columns],
                send_sem=send_sem.at[flow, c],
                recv_sem=sems.at[section, c],
                device_id=device,
                device_id_type=MESH,
            )

        return [chunk(c) for c in range(CHUNKS)]

    own = pixels_ref.at[0]
    above, before = {"strip": strip - 1}, {"sec": sec - 1}
    near_send = remote(0, own, main_ref, main_sem, 1, before)
    rim_send = remote(1, own, rim_ref, rim_sem, 0, above)
    diagonal_send = remote(2, own, rim_ref, rim_sem, 1, {"sec": sec - 1, "strip": strip - 1})
    routed_send = remote(3, own, main_ref, main_sem, 2, {"sec": sec - 2})
    far_relay = remote(4, main_ref.at[1], main_ref, main_sem, 2, before)
    near_rim_relay = remote(5, main_ref.at[1], rim_ref, rim_sem, 1, above)
    far_rim_relay = remote(6, rim_ref.at[1], rim_ref, rim_sem, 2, before)
    far_rim_across = remote(7, main_ref.at[2], rim_ref, rim_sem, 2, above)

    def each(condition, copies, method):
        @pl.when(condition)
        def _():
            for copy in copies:
                getattr(copy, method)()

    each(diagonal, diagonal_send, "start")
    each(routed, routed_send, "start")
    each(sec >= 1, near_send, "start")
    each(strip >= 1, rim_send, "start")

    @pl.when(jnp.logical_not(below))
    def _():
        rim_ref[...] = jnp.zeros_like(rim_ref)

    sums_ref[...] = jnp.zeros_like(sums_ref)

    fine_rows, fine_cols = fine_mask_ref.shape[1:]
    coarse_rows, coarse_cols = coarse_mask_ref.shape[1:]
    fine_groups = fine_rows * fine_cols // 4
    count = fine_groups + coarse_rows * coarse_cols // 4
    (
        first_ref,
        fine_high_ref,
        fine_low_ref,
        coarse_high_ref,
        coarse_low_ref,
        inverse_high_ref,
        inverse_low_ref,
        last_ref,
        energy_ref,
        weight_ref,
    ) = held

    def spread(mask, cols):
        source = lax.broadcasted_iota(jnp.int32, (cols, cols * WINDOW), 0)
        target = lax.broadcasted_iota(jnp.int32, (cols, cols * WINDOW), 1) // WINDOW
        picks = jnp.where(source == target, 1.0, 0.0).astype(BF16)
        return matmul(mask.astype(F32).astype(BF16), picks)

    fine_mask = spread(fine_mask_ref[0], fine_cols)
    coarse_mask = spread(coarse_mask_ref[0], coarse_cols)
    masks = [
        m[r : r + 1, LANES * t : LANES * (t + 1)]
        for m in (fine_mask, coarse_mask)
        for r in range(m.shape[0])
        for t in range(m.shape[1] // LANES)
    ]

    def analyse(section):
        weight = jnp.concatenate([weight_ref[...]] * 2, axis=1)
        real, imag = section_spectra(
            jnp.concatenate([main_ref[section], rim_ref[section]], axis=0),
            first_ref[...],
            (fine_high_ref[...], fine_low_ref[...]),
            (coarse_high_ref[...], coarse_low_ref[...]),
            fine_rows,
            coarse_rows,
        )
        for g in range(count):
            real_ref[section, KP * g : KP * (g + 1)] = real[g]
            imag_ref[section, KP * g : KP * (g + 1)] = imag[g]
            power = weight * (real[g] * real[g] + imag[g] * imag[g])
            sums_ref[section, g : g + 1] = jnp.sum(power, axis=0, keepdims=True)
        total = jnp.dot(
            sums_ref[section], energy_ref[...], preferred_element_type=F32, precision=lax.Precision.HIGHEST
        )
        scale_ref[section] = 1.0 / jnp.sqrt(total * (1.0 / float(PATCH) ** 4) + 1e-05)

    def correlate(d):
        cross_real = real_ref[0] * real_ref[d] + imag_ref[0] * imag_ref[d]
        cross_imag = real_ref[0] * imag_ref[d] - imag_ref[0] * real_ref[d]
        cross = jnp.concatenate([cross_real.astype(BF16), cross_imag.astype(BF16)], axis=1)
        rows = matmul(cross, inverse_high_ref[...]) + matmul(cross, inverse_low_ref[...])
        stacked = []
        for g in range(count):
            part = rows[KP * g : KP * (g + 1)]
            stacked.append(jnp.concatenate([part[:, :LANES], part[:, LANES:]], axis=0))
        high, low = split_value(jnp.concatenate(stacked, axis=1))
        maps = matmul(last_ref[...], jnp.concatenate([high, low, high], axis=0))
        both = scale_ref[0] * scale_ref[d] * (1.0 / float(PATCH) ** 3)
        for g in range(count):
            scale = both[g : g + 1] * masks[g]
            value = block_transpose(maps[:, LANES * g : LANES * (g + 1)] * scale)
            if g < fine_groups:
                ref, local_g, cols = fine_out_ref, g, fine_cols
            else:
                ref, local_g, cols = coarse_out_ref, g - fine_groups, coarse_cols
            i, j = divmod(4 * local_g, cols)
            for q in range(WINDOW // 4):
                ref[0, d - 1, i, j : j + 4, LANES * q : LANES * (q + 1)] = value[4 * q : 4 * (q + 1)]

    def clear(d):
        for ref in (fine_out_ref, coarse_out_ref):
            ref[0, d - 1] = jnp.zeros(ref.shape[2:], F32)

    own_copy.wait()
    for copy in const_copies:
        copy.wait()
    each(below, rim_send, "wait_recv")
    analyse(0)

    @pl.when(has_near)
    def _():
        for c in range(CHUNKS):
            near_send[c].wait_recv()
            pl.when(odd & (sec >= 1))(far_relay[c].start)
            pl.when(odd)(near_rim_relay[c].start)

        @pl.when(below)
        def _():
            for c in range(CHUNKS):
                near_rim_relay[c].wait_recv()
                pl.when(odd & (sec >= 1))(far_rim_relay[c].start)

        analyse(1)

    @pl.when(has_far)
    def _():
        for c in range(CHUNKS):
            far_relay[c].wait_recv()
            pl.when(odd)(far_rim_across[c].start)

    @pl.when(has_near)
    def _():
        correlate(1)

    @pl.when(has_far)
    def _():
        each(below, far_rim_relay, "wait_recv")
        analyse(2)
        correlate(2)

    pl.when(jnp.logical_not(has_near))(lambda: clear(1))
    pl.when(jnp.logical_not(has_far))(lambda: clear(2))
    each(sec >= 1, near_send, "wait_send")
    each(strip >= 1, rim_send, "wait_send")
    each(diagonal, diagonal_send, "wait_send")
    each(routed, routed_send, "wait_send")
    each(odd & has_near & (sec >= 1), far_relay, "wait_send")
    each(odd & has_near, near_rim_relay, "wait_send")
    each(odd & has_near & below & (sec >= 1), far_rim_relay, "wait_send")
    each(odd & has_far, far_rim_across, "wait_send")


def deliver(fine_ref, coarse_ref, fine_out_ref, coarse_out_ref, sem):
    copies = [
        pltpu.make_async_copy(source.at[0, d], target.at[0, d], sem.at[index, d])
        for index, (source, target) in enumerate(((fine_ref, fine_out_ref), (coarse_ref, coarse_out_ref)))
        for d in range(2)
    ]
    for copy in copies:
        copy.start()
    for copy in copies:
        copy.wait()


def local(sections, mask_fine, mask_coarse):
    strip_rows, width = sections.shape[1:]
    consts = [jnp.asarray(t) for t in tables(strip_rows)]
    fine_rows, fine_cols = mask_fine.shape[1:]
    coarse_rows, coarse_cols = mask_coarse.shape[1:]
    count = (fine_rows * fine_cols + coarse_rows * coarse_cols) // 4
    vmem = pl.BlockSpec(memory_space=pltpu.VMEM)
    anywhere = pl.BlockSpec(memory_space=pl.ANY)
    flat = WINDOW * WINDOW
    sums = -(-count // 8) * 8
    shapes = (
        jax.ShapeDtypeStruct((1, 2, fine_rows, fine_cols, flat), F32),
        jax.ShapeDtypeStruct((1, 2, coarse_rows, coarse_cols, flat), F32),
    )
    operands = [pltpu.with_memory_space_constraint(t, pltpu.HBM) for t in (sections, mask_fine, mask_coarse, *consts)]
    maps = pl.pallas_call(
        functools.partial(compute, len(consts)),
        out_shape=shapes,
        in_specs=[anywhere, vmem, vmem] + [anywhere] * len(consts),
        out_specs=(vmem, vmem),
        scratch_shapes=[
            pltpu.VMEM((3, strip_rows, width), BF16),
            pltpu.VMEM((3, strip_rows, width), BF16),
            pltpu.VMEM((3, KP * count, 2 * LANES), F32),
            pltpu.VMEM((3, KP * count, 2 * LANES), F32),
            pltpu.VMEM((3, sums, 2 * LANES), F32),
            pltpu.VMEM((3, sums, LANES), F32),
            *[pltpu.VMEM(c.shape, c.dtype) for c in consts],
            pltpu.SemaphoreType.DMA,
            pltpu.SemaphoreType.DMA((len(consts),)),
            pltpu.SemaphoreType.DMA((8, CHUNKS)),
            pltpu.SemaphoreType.DMA((3, CHUNKS)),
            pltpu.SemaphoreType.DMA((3, CHUNKS)),
        ],
        compiler_params=pltpu.CompilerParams(collective_id=0, has_side_effects=True, vmem_limit_bytes=GRANT),
    )(*operands)
    return pl.pallas_call(
        deliver,
        out_shape=shapes,
        in_specs=[vmem, vmem],
        out_specs=(anywhere, anywhere),
        scratch_shapes=[pltpu.SemaphoreType.DMA((2, 2))],
        compiler_params=pltpu.CompilerParams(vmem_limit_bytes=GRANT),
    )(*maps)


def solution(mesh):
    in_specs = (
        P("sec", "strip", "groups"),
        P("sec", "strip", "groups"),
        P("sec", "strip", "groups"),
    )
    out_specs = (P("sec", None, "strip", "groups", None), P("sec", None, "strip", "groups", None))
    return jax.shard_map(local, mesh=mesh, in_specs=in_specs, out_specs=out_specs, check_vma=False)
```

```python
import functools

import jax
import jax.numpy as jnp
import numpy as np
from jax import lax
from jax.experimental import pallas as pl
from jax.experimental.pallas import tpu as pltpu
from jax.sharding import PartitionSpec as P

PATCH = 64
STRIDE = 32
WINDOW = 32
HALF = PATCH // 2 + 1
KP = 40
CHUNKS = 2
TABLE_SCALE = 1.869
GRANT = 48 * 1024 * 1024
LANES = 128
F32 = jnp.float32
BF16 = jnp.bfloat16
MESH = pl.DeviceIdType.MESH


def trig(phase):
    angle = 2.0 * np.pi / PATCH * np.mod(phase, PATCH)
    return np.round(np.cos(angle), 12), np.round(np.sin(angle), 12)


def split(table):
    high = np.asarray(table, np.float32).astype(BF16)
    low = (np.asarray(table, np.float64) - high.astype(np.float64)).astype(np.float32).astype(BF16)
    return high, low


def block_diagonal(block, count):
    return np.kron(np.eye(count), block)


def rounded(table):
    scaled = np.asarray(table, np.float64) * TABLE_SCALE
    return scaled.astype(np.float32).astype(BF16)


def table_gain():
    c, _ = trig(np.arange(PATCH))
    return float(c @ rounded(c).astype(np.float64) / (c @ c))


def inner_rows(strip_rows):
    return len([i for i in range(strip_rows // STRIDE) if STRIDE * i + PATCH <= strip_rows])


def tables(strip_rows):
    fine_rows = strip_rows // STRIDE
    coarse_rows = strip_rows // (2 * STRIDE)
    inner = inner_rows(strip_rows)
    height = strip_rows + PATCH
    k = np.arange(KP)[:, None]
    keep = (k < HALF).astype(np.float64)
    x = np.arange(height)[None, :]
    units = []
    for i in range(fine_rows):
        c, s = trig(k * (x - STRIDE * i))
        inside = ((x >= STRIDE * i) & (x < STRIDE * i + PATCH)) * keep
        units += [c * inside, -s * inside]
    for i in range(coarse_rows):
        xc = x // 2 - STRIDE * i
        c, s = trig(k * xc)
        inside = ((xc >= 0) & (xc < PATCH)) * keep * 0.25
        units += [c * inside, -s * inside]

    def first(parts, rows):
        high, low = split(np.concatenate(parts, axis=0)[:, :rows])
        return np.concatenate([high, low], axis=1)

    firsts = [first(units[2 * inner :], height)]
    if inner:
        firsts.insert(0, first(units[: 2 * inner], strip_rows))

    freq = np.arange(PATCH)[None, :]
    y = np.arange(STRIDE)[:, None]
    c, s = trig(y * freq)

    def second(c, s, count):
        c, s = block_diagonal(c, count), block_diagonal(s, count)
        return rounded(np.block([[c, -s], [s, c]]))

    fine_w = second(c, s, LANES // STRIDE)
    coarse_w = second(np.repeat(c, 2, axis=0), np.repeat(s, 2, axis=0), LANES // (2 * STRIDE))

    shift = np.arange(WINDOW) - WINDOW // 2
    c, s = trig(np.arange(PATCH)[:, None] * shift[None, :])
    c, s = block_diagonal(c, 4), block_diagonal(s, 4)
    inverse = rounded(np.block([[c, s], [-s, c]]))

    weight = np.where((k == 0) | (k == PATCH // 2), 1.0, 2.0) * keep
    c, s = trig(shift[:, None] * np.arange(KP)[None, :])
    last_high, last_low = split(np.concatenate([c * weight.T, -s * weight.T], axis=1))
    last = np.concatenate([last_high, last_high, last_low], axis=1)
    energy = np.kron(np.eye(4), np.ones((PATCH, WINDOW)))
    return [
        fine_w,
        coarse_w,
        inverse,
        last,
        np.asarray(energy, np.float32).astype(BF16),
        np.asarray(np.broadcast_to(weight, (KP, LANES)), np.float32),
        *firsts,
    ]


def split_value(value):
    high = value.astype(BF16)
    return high, (value - high.astype(F32)).astype(BF16)


def matmul(a, b):
    return jnp.dot(a, b, preferred_element_type=F32)


def section_spectra(pixels, first, fine_w, coarse_w, fine_rows, coarse_rows):
    half = matmul(first, jnp.concatenate([pixels, pixels], axis=0))
    width = half.shape[1]
    tiles = width // LANES
    row = lax.broadcasted_iota(jnp.int32, (KP, width), 0)
    fine_in, coarse_in = [], []
    for unit in range(fine_rows + coarse_rows):
        real = half[2 * KP * unit : 2 * KP * unit + KP]
        imag = half[2 * KP * unit + KP : 2 * KP * (unit + 1)]
        sums = real[0:1]
        high = sums.astype(BF16).astype(F32)
        middle = (sums - high).astype(BF16).astype(F32)
        low = sums - high - middle
        real = jnp.where(row == 0, high, real)
        real = jnp.where(row == HALF, middle, real)
        real = jnp.where(row == HALF + 1, low, real)
        target = fine_in if unit < fine_rows else coarse_in
        for tile in range(tiles):
            at = slice(LANES * tile, LANES * (tile + 1))
            target.append(jnp.concatenate([real[:, at], imag[:, at]], axis=1))

    def transform(parts, weights):
        high, low = split_value(jnp.concatenate(parts, axis=0))
        return matmul(high, weights) + matmul(low, weights)

    fine = transform(fine_in, fine_w) if fine_rows else None
    coarse = transform(coarse_in, coarse_w) if coarse_rows else None
    wide = 2 * LANES
    lane = lax.broadcasted_iota(jnp.int32, (KP, wide), 1)
    krow = lax.broadcasted_iota(jnp.int32, (KP, wide), 0)
    sign = jnp.where(lane % 2 == 0, 1.0, -1.0).astype(F32)
    dc = (krow == 0) & (lane % PATCH == 0)

    def finish(parts, rows):
        count = len(parts) // rows
        rolled = [pltpu.roll(part, wide - PATCH, 1) for part in parts]
        done = []
        for index, part in enumerate(parts):
            if index % count == count - 1:
                following = jnp.where(lane < wide - PATCH, rolled[index], 0.0)
            else:
                following = jnp.where(lane < wide - PATCH, rolled[index], rolled[index + 1])
            value = part + sign * following
            value = jnp.where(krow == 0, value + value[HALF : HALF + 1] + value[HALF + 1 : HALF + 2], value)
            value = jnp.where(dc, 0.0, value)
            done.append(value)
        return done

    def groups(offset):
        fine_parts = [
            fine[KP * g : KP * (g + 1), offset * wide : (offset + 1) * wide]
            for g in range(fine_rows * tiles)
        ]
        coarse_parts = [
            jnp.concatenate(
                [
                    coarse[KP * g : KP * (g + 1), offset * LANES : (offset + 1) * LANES],
                    coarse[KP * (g + 1) : KP * (g + 2), offset * LANES : (offset + 1) * LANES],
                ],
                axis=1,
            )
            for g in range(0, coarse_rows * tiles, 2)
        ]
        done = finish(fine_parts, fine_rows) if fine_rows else []
        return done + (finish(coarse_parts, coarse_rows) if coarse_rows else [])

    return groups(0), groups(1)


def block_transpose(value):
    row = lax.broadcasted_iota(jnp.int32, value.shape, 0) % 4
    block = lax.broadcasted_iota(jnp.int32, value.shape, 1) // WINDOW
    rows = value.shape[0]
    moved = pltpu.roll(value, 2 * WINDOW, 1)
    other = jnp.where(row < 2, pltpu.roll(moved, rows - 2, 0), pltpu.roll(moved, 2, 0))
    value = jnp.where((row // 2) == (block // 2), value, other)
    right = pltpu.roll(pltpu.roll(value, WINDOW, 1), rows - 1, 0)
    left = pltpu.roll(pltpu.roll(value, LANES - WINDOW, 1), 1, 0)
    other = jnp.where(row % 2 == 0, right, left)
    return jnp.where((row % 2) == (block % 2), value, other)


def compute(const_count, *refs):
    pixels_ref, fine_mask_ref, coarse_mask_ref = refs[:3]
    sources = refs[3 : 3 + const_count]
    fine_out_ref, coarse_out_ref = refs[3 + const_count : 5 + const_count]
    main_ref, rim_ref, real_ref, imag_ref, scale_ref = refs[5 + const_count : 10 + const_count]
    held = refs[10 + const_count : 10 + 2 * const_count]
    own_sem, const_sem, send_sem, main_sem, rim_sem = refs[10 + 2 * const_count :]
    sec, strip = lax.axis_index("sec"), lax.axis_index("strip")
    secs, strips = lax.axis_size("sec"), lax.axis_size("strip")
    even, odd = strip % 2 == 0, strip % 2 == 1
    below = strip + 1 < strips
    has_near, has_far = sec + 1 < secs, sec + 2 < secs

    barrier = pltpu.get_barrier_semaphore()

    def greet(condition, device):
        @pl.when(condition)
        def _():
            pl.semaphore_signal(barrier, inc=1, device_id=device, device_id_type=MESH)

    greet(even & has_far, {"sec": sec + 2})
    greet(odd & has_near & below, {"sec": sec + 1, "strip": strip + 1})
    greet(has_near, {"sec": sec + 1})
    greet(below, {"strip": strip + 1})

    own_copy = pltpu.make_async_copy(pixels_ref.at[0], main_ref.at[0], own_sem)
    own_copy.start()
    const_copies = [
        pltpu.make_async_copy(source, target, const_sem.at[index])
        for index, (source, target) in enumerate(zip(sources, held))
    ]
    for copy in const_copies:
        copy.start()

    diagonal = even & (sec >= 1) & (strip >= 1)
    routed = even & (sec >= 2)
    one = lambda condition: jnp.where(condition, 1, 0)
    targets = one(sec >= 1) + one(strip >= 1) + one(diagonal) + one(routed)

    @pl.when(targets >= 1)
    def _():
        pl.semaphore_wait(barrier, targets)

    piece = pixels_ref.shape[2] // CHUNKS

    def remote(flow, source, target, sems, section, device):
        def chunk(c):
            columns = (slice(None), pl.ds(piece * c, piece))
            return pltpu.make_async_remote_copy(
                src_ref=source.at[columns],
                dst_ref=target.at[section].at[columns],
                send_sem=send_sem.at[flow, c],
                recv_sem=sems.at[section, c],
                device_id=device,
                device_id_type=MESH,
            )

        return [chunk(c) for c in range(CHUNKS)]

    own = pixels_ref.at[0]
    above, before = {"strip": strip - 1}, {"sec": sec - 1}
    near_send = remote(0, own, main_ref, main_sem, 1, before)
    rim_send = remote(1, own, rim_ref, rim_sem, 0, above)
    diagonal_send = remote(2, own, rim_ref, rim_sem, 1, {"sec": sec - 1, "strip": strip - 1})
    routed_send = remote(3, own, main_ref, main_sem, 2, {"sec": sec - 2})
    far_relay = remote(4, main_ref.at[1], main_ref, main_sem, 2, before)
    near_rim_relay = remote(5, main_ref.at[1], rim_ref, rim_sem, 1, above)
    far_rim_relay = remote(6, rim_ref.at[1], rim_ref, rim_sem, 2, before)
    far_rim_across = remote(7, main_ref.at[2], rim_ref, rim_sem, 2, above)

    def each(condition, copies, method):
        @pl.when(condition)
        def _():
            for copy in copies:
                getattr(copy, method)()

    each(strip >= 1, rim_send, "start")
    each(diagonal, diagonal_send, "start")
    each(sec >= 1, near_send, "start")
    each(routed, routed_send, "start")

    @pl.when(jnp.logical_not(below))
    def _():
        rim_ref[...] = jnp.zeros_like(rim_ref)

    fine_rows, fine_cols = fine_mask_ref.shape[1:]
    coarse_rows, coarse_cols = coarse_mask_ref.shape[1:]
    fine_groups = fine_rows * fine_cols // 4
    count = fine_groups + coarse_rows * coarse_cols // 4
    fine_w_ref, coarse_w_ref, inverse_ref, last_ref, energy_ref, weight_ref = held[:6]
    first_refs = held[6:]
    inner = inner_rows(pixels_ref.shape[1])
    inner_groups = inner * fine_cols // 4
    bounds = {"inner": (0, inner_groups), "outer": (inner_groups, count)}
    gain = table_gain()

    def spread(mask, cols):
        source = lax.broadcasted_iota(jnp.int32, (cols, cols * WINDOW), 0)
        target = lax.broadcasted_iota(jnp.int32, (cols, cols * WINDOW), 1) // WINDOW
        picks = jnp.where(source == target, 1.0, 0.0).astype(BF16)
        return matmul(mask.astype(F32).astype(BF16), picks)

    fine_mask = spread(fine_mask_ref[0], fine_cols)
    coarse_mask = spread(coarse_mask_ref[0], coarse_cols)
    masks = [
        m[r : r + 1, LANES * t : LANES * (t + 1)]
        for m in (fine_mask, coarse_mask)
        for r in range(m.shape[0])
        for t in range(m.shape[1] // LANES)
    ]

    def analyse(section, part):
        start, stop = bounds[part]
        if start == stop:
            return
        weight = jnp.concatenate([weight_ref[...]] * 2, axis=1)
        if part == "inner":
            pixels, rows = main_ref[section], (inner, 0)
        else:
            pixels = jnp.concatenate([main_ref[section], rim_ref[section]], axis=0)
            rows = (fine_rows - inner, coarse_rows)
        first = first_refs[0 if part == "inner" else -1][...]
        real, imag = section_spectra(pixels, first, fine_w_ref[...], coarse_w_ref[...], *rows)
        sums = []
        for g in range(start, stop):
            re, im = real[g - start], imag[g - start]
            real_ref[section, KP * g : KP * (g + 1)] = re
            imag_ref[section, KP * g : KP * (g + 1)] = im
            sums.append(jnp.sum(weight * (re * re + im * im), axis=0, keepdims=True))
        sums = jnp.concatenate(sums, axis=0)
        high, rest = split_value(sums)
        low = (sums - high.astype(F32) - rest.astype(F32)).astype(BF16)
        energy = energy_ref[...]
        total = matmul(high, energy) + matmul(rest, energy) + matmul(low, energy)
        scale = 1.0 / jnp.sqrt(total * (1.0 / (float(PATCH) ** 4 * gain * gain)) + 1e-05)
        scale_ref[section, start:stop] = scale

    def correlate(d, part):
        start, stop = bounds[part]
        if start == stop:
            return
        rows = slice(KP * start, KP * stop)
        own_real, own_imag = real_ref[0, rows], imag_ref[0, rows]
        other_real, other_imag = real_ref[d, rows], imag_ref[d, rows]
        cross_real = own_real * other_real + own_imag * other_imag
        cross_imag = own_real * other_imag - own_imag * other_real
        cross = jnp.concatenate([cross_real.astype(BF16), cross_imag.astype(BF16)], axis=1)
        rows = matmul(cross, inverse_ref[...])
        stacked = []
        for g in range(stop - start):
            piece = rows[KP * g : KP * (g + 1)]
            stacked.append(jnp.concatenate([piece[:, :LANES], piece[:, LANES:]], axis=0))
        high, low = split_value(jnp.concatenate(stacked, axis=1))
        maps = matmul(last_ref[...], jnp.concatenate([high, low, high], axis=0))
        both = scale_ref[0, start:stop] * scale_ref[d, start:stop] * (1.0 / (float(PATCH) ** 3 * gain**3))
        for g in range(start, stop):
            at = g - start
            scale = both[at : at + 1] * masks[g]
            value = block_transpose(maps[:, LANES * at : LANES * (at + 1)] * scale)
            if g < fine_groups:
                ref, local_g, cols = fine_out_ref, g, fine_cols
            else:
                ref, local_g, cols = coarse_out_ref, g - fine_groups, coarse_cols
            i, j = divmod(4 * local_g, cols)
            for q in range(WINDOW // 4):
                ref[0, d - 1, i, j : j + 4, LANES * q : LANES * (q + 1)] = value[4 * q : 4 * (q + 1)]

    def clear(d):
        for ref in (fine_out_ref, coarse_out_ref):
            ref[0, d - 1] = jnp.zeros(ref.shape[2:], F32)

    own_copy.wait()
    for copy in const_copies:
        copy.wait()
    analyse(0, "inner")
    @pl.when(has_near)
    def _():
        for c in range(CHUNKS):
            near_send[c].wait_recv()
            pl.when(odd & (sec >= 1))(far_relay[c].start)
            pl.when(odd)(near_rim_relay[c].start)

    each(below, rim_send, "wait_recv")
    analyse(0, "outer")

    @pl.when(has_near)
    def _():
        @pl.when(below)
        def _():
            for c in range(CHUNKS):
                near_rim_relay[c].wait_recv()
                pl.when(odd & (sec >= 1))(far_rim_relay[c].start)

        analyse(1, "inner")
        analyse(1, "outer")

    @pl.when(has_far)
    def _():
        for c in range(CHUNKS):
            far_relay[c].wait_recv()
            pl.when(odd)(far_rim_across[c].start)

    @pl.when(has_near)
    def _():
        correlate(1, "inner")
        correlate(1, "outer")

    @pl.when(has_far)
    def _():
        analyse(2, "inner")
        correlate(2, "inner")
        each(below, far_rim_relay, "wait_recv")
        analyse(2, "outer")
        correlate(2, "outer")

    pl.when(jnp.logical_not(has_near))(lambda: clear(1))
    pl.when(jnp.logical_not(has_far))(lambda: clear(2))
    each(sec >= 1, near_send, "wait_send")
    each(strip >= 1, rim_send, "wait_send")
    each(diagonal, diagonal_send, "wait_send")
    each(routed, routed_send, "wait_send")
    each(odd & has_near & (sec >= 1), far_relay, "wait_send")
    each(odd & has_near, near_rim_relay, "wait_send")
    each(odd & has_near & below & (sec >= 1), far_rim_relay, "wait_send")
    each(odd & has_far, far_rim_across, "wait_send")


def deliver(fine_ref, coarse_ref, fine_out_ref, coarse_out_ref, sem):
    copies = [
        pltpu.make_async_copy(source.at[0, d], target.at[0, d], sem.at[index, d])
        for index, (source, target) in enumerate(((fine_ref, fine_out_ref), (coarse_ref, coarse_out_ref)))
        for d in range(2)
    ]
    for copy in copies:
        copy.start()
    for copy in copies:
        copy.wait()


def local(sections, mask_fine, mask_coarse):
    strip_rows, width = sections.shape[1:]
    consts = [jnp.asarray(t) for t in tables(strip_rows)]
    fine_rows, fine_cols = mask_fine.shape[1:]
    coarse_rows, coarse_cols = mask_coarse.shape[1:]
    count = (fine_rows * fine_cols + coarse_rows * coarse_cols) // 4
    vmem = pl.BlockSpec(memory_space=pltpu.VMEM)
    anywhere = pl.BlockSpec(memory_space=pl.ANY)
    flat = WINDOW * WINDOW
    shapes = (
        jax.ShapeDtypeStruct((1, 2, fine_rows, fine_cols, flat), F32),
        jax.ShapeDtypeStruct((1, 2, coarse_rows, coarse_cols, flat), F32),
    )
    operands = [pltpu.with_memory_space_constraint(t, pltpu.HBM) for t in (sections, mask_fine, mask_coarse, *consts)]
    maps = pl.pallas_call(
        functools.partial(compute, len(consts)),
        out_shape=shapes,
        in_specs=[anywhere, vmem, vmem] + [anywhere] * len(consts),
        out_specs=(vmem, vmem),
        scratch_shapes=[
            pltpu.VMEM((3, strip_rows, width), BF16),
            pltpu.VMEM((3, strip_rows, width), BF16),
            pltpu.VMEM((3, KP * count, 2 * LANES), F32),
            pltpu.VMEM((3, KP * count, 2 * LANES), F32),
            pltpu.VMEM((3, count, LANES), F32),
            *[pltpu.VMEM(c.shape, c.dtype) for c in consts],
            pltpu.SemaphoreType.DMA,
            pltpu.SemaphoreType.DMA((len(consts),)),
            pltpu.SemaphoreType.DMA((8, CHUNKS)),
            pltpu.SemaphoreType.DMA((3, CHUNKS)),
            pltpu.SemaphoreType.DMA((3, CHUNKS)),
        ],
        compiler_params=pltpu.CompilerParams(collective_id=0, has_side_effects=True, vmem_limit_bytes=GRANT),
    )(*operands)
    return pl.pallas_call(
        deliver,
        out_shape=shapes,
        in_specs=[vmem, vmem],
        out_specs=(anywhere, anywhere),
        scratch_shapes=[pltpu.SemaphoreType.DMA((2, 2))],
        compiler_params=pltpu.CompilerParams(vmem_limit_bytes=GRANT),
    )(*maps)


def solution(mesh):
    in_specs = (
        P("sec", "strip", "groups"),
        P("sec", "strip", "groups"),
        P("sec", "strip", "groups"),
    )
    out_specs = (P("sec", None, "strip", "groups", None), P("sec", None, "strip", "groups", None))
    return jax.shard_map(local, mesh=mesh, in_specs=in_specs, out_specs=out_specs, check_vma=False)
```

```python
import functools

import jax
import jax.numpy as jnp
import numpy as np
from jax import lax
from jax.experimental import pallas as pl
from jax.experimental.pallas import tpu as pltpu
from jax.sharding import PartitionSpec as P

PATCH = 64
STRIDE = 32
WINDOW = 32
SLOTS = PATCH // 2
CHUNKS = 2
TABLE_SCALE = 1.869
GRANT = 48 * 1024 * 1024
LANES = 128
F32 = jnp.float32
BF16 = jnp.bfloat16
MESH = pl.DeviceIdType.MESH


def trig(phase):
    angle = 2.0 * np.pi / PATCH * np.mod(phase, PATCH)
    return np.round(np.cos(angle), 12), np.round(np.sin(angle), 12)


def split(table):
    high = np.asarray(table, np.float32).astype(BF16)
    low = (np.asarray(table, np.float64) - high.astype(np.float64)).astype(np.float32).astype(BF16)
    return high, low


def block_diagonal(block, count):
    return np.kron(np.eye(count), block)


def rounded(table):
    scaled = np.asarray(table, np.float64) * TABLE_SCALE
    return scaled.astype(np.float32).astype(BF16)


def table_gain():
    c, _ = trig(np.arange(PATCH))
    return float(c @ rounded(c).astype(np.float64) / (c @ c))


def inner_rows(strip_rows):
    return len([i for i in range(strip_rows // STRIDE) if STRIDE * i + PATCH <= strip_rows])


def tables(strip_rows):
    fine_rows = strip_rows // STRIDE
    coarse_rows = strip_rows // (2 * STRIDE)
    inner = inner_rows(strip_rows)
    height = strip_rows + PATCH
    k = np.concatenate([[PATCH // 2], np.arange(1, SLOTS)])[:, None]
    x = np.arange(height)[None, :]
    units, sums = [], []
    for i in range(fine_rows):
        inside = ((x >= STRIDE * i) & (x < STRIDE * i + PATCH)) * 1.0
        c, s = trig(k * (x - STRIDE * i))
        units.append(np.concatenate([c * inside, -s * inside]))
        sums.append(np.repeat(inside, 8, axis=0))
    for i in range(coarse_rows):
        xc = x // 2 - STRIDE * i
        inside = ((xc >= 0) & (xc < PATCH)) * 0.25
        c, s = trig(k * xc)
        units.append(np.concatenate([c * inside, -s * inside]))
        sums.append(np.repeat(inside, 8, axis=0))

    def first(at, rows):
        high, low = split(np.concatenate(units[at] + sums[at], axis=0)[:, :rows])
        return np.concatenate([high, low], axis=1)

    firsts = [first(slice(inner, None), height)]
    if inner:
        firsts.insert(0, first(slice(0, inner), strip_rows))

    lane = np.arange(LANES)
    half, quarter = LANES // 2, LANES // 4
    middle = (lane >= quarter) & (lane < 3 * quarter)
    windows = [
        (lane % half, lane >= half),
        (np.where(middle, lane - quarter, np.where(lane < quarter, lane + quarter, lane - 3 * quarter)), ~middle),
        (lane % half, lane < half),
        (np.where(lane < quarter, lane + quarter, np.where(middle, lane - quarter, lane - 3 * quarter)), middle),
    ]
    freq = np.arange(PATCH)[None, :]

    def weights(y, is_imag):
        c, s = trig(y[:, None] * freq)
        from_real = np.concatenate([c, -s, -s, -c], axis=1)
        from_imag = np.concatenate([s, c, c, -s], axis=1)
        return rounded(np.where(is_imag[:, None], from_imag, from_real))

    fine_w = np.concatenate([np.concatenate([weights(*w)] * 2, axis=0) for w in windows], axis=0)
    both = np.arange(2 * LANES) >= LANES
    coarse_w = np.concatenate(
        [weights(np.concatenate([at // 2] * 2), both) for at in (lane, (lane + half) % LANES)], axis=0
    )

    shift = np.arange(WINDOW) - WINDOW // 2
    c, s = trig((np.arange(LANES) % PATCH)[:, None] * shift[None, :])
    inverse = []
    for p in range(4):
        block = np.zeros((2 * LANES, 2 * LANES))
        block[:LANES, WINDOW * p : WINDOW * (p + 1)] = c
        block[:LANES, LANES + WINDOW * p : LANES + WINDOW * (p + 1)] = s
        block[LANES:, WINDOW * p : WINDOW * (p + 1)] = -s
        block[LANES:, LANES + WINDOW * p : LANES + WINDOW * (p + 1)] = c
        inverse.append(rounded(block))

    weight = np.where(k == PATCH // 2, 1.0, 2.0)
    c, s = trig(shift[:, None] * k.T)
    last_high, last_low = split(np.concatenate([c * weight.T, -s * weight.T], axis=1))
    last = np.concatenate([last_high, last_high, last_low], axis=1)
    return [fine_w, coarse_w, np.concatenate(inverse, axis=0), last, *firsts]


def split_value(value):
    high = value.astype(BF16)
    return high, (value - high.astype(F32)).astype(BF16)


def matmul(a, b):
    return jnp.dot(a, b, preferred_element_type=F32)


def lanes_of(shape):
    return lax.broadcasted_iota(jnp.int32, shape, 1)


def rows_of(shape):
    return lax.broadcasted_iota(jnp.int32, shape, 0)


def tiles_of(value):
    return [value[:, LANES * t : LANES * (t + 1)] for t in range(value.shape[1] // LANES)]


def window(kind, real, turned, real_next, turned_next):
    lane = lanes_of(real.shape)
    half, quarter = LANES // 2, LANES // 4
    if kind == 0:
        return jnp.where(lane < half, real, turned)
    if kind == 1:
        return jnp.where((lane >= quarter) & (lane < 3 * quarter), real, turned)
    if kind == 2:
        return jnp.where(lane < half, turned, real)
    left = jnp.where(lane < quarter, real_next, turned)
    right = jnp.where(lane < 3 * quarter, turned_next, real)
    return jnp.where(lane < half, left, right)


def sum_rows(value):
    row = rows_of((8, LANES))
    tiles = tiles_of(value)
    tiles.append(jnp.zeros_like(tiles[0]))
    count = len(tiles) - 1

    def spread(parts):
        out = parts[count - 1]
        for t in range(count - 1):
            out = jnp.where(row % count == t, parts[t], out)
        return out

    return spread(tiles[:-1]), spread(tiles[1:])


def sum_parts(value, count):
    first = rows_of(value.shape) < count
    high, rest = split_value(value)
    high = high.astype(F32)
    middle = rest.astype(F32)
    low = value - high - middle
    return jnp.where(first, high, low).astype(BF16), jnp.where(first, middle, 0.0).astype(BF16)


def section_spectra(pixels, first, fine_w_ref, coarse_w_ref, fine_rows, coarse_rows, columns):
    rows = matmul(first, jnp.concatenate([pixels, pixels], axis=0))
    units = fine_rows + coarse_rows
    count = rows.shape[1] // LANES
    zero = jnp.zeros((SLOTS, LANES), BF16)
    blank = jnp.zeros((8, LANES), F32)
    done = []

    def finish(out):
        sums = out[SLOTS * count : SLOTS * count + 8]
        sums = sums + pltpu.roll(sums, 4, 0)
        sums = jnp.where(lanes_of(sums.shape) % PATCH == 0, 0.0, sums)
        done.append((out, sums))

    for unit in range(units):
        real = tiles_of(rows[2 * SLOTS * unit : 2 * SLOTS * unit + SLOTS])
        imag = tiles_of(rows[2 * SLOTS * unit + SLOTS : 2 * SLOTS * (unit + 1)])
        if unit < fine_rows:
            imag = [pltpu.roll(tile, LANES // 2, 1) for tile in imag]
        real = [split_value(tile) for tile in real] + [(zero, zero)]
        imag = [split_value(tile) for tile in imag] + [(zero, zero)]
        at = 2 * SLOTS * units + 8 * unit
        now, following = sum_rows(rows[at : at + 8])
        if unit < fine_rows:
            for kind in range(4):
                lhs = [
                    jnp.concatenate(
                        [window(kind, real[t][h], imag[t][h], real[t + 1][h], imag[t + 1][h]) for h in range(2)], axis=1
                    )
                    for t in range(count)
                ]
                sums = sum_parts(window(kind, now, blank, following, blank), count)
                lhs.append(jnp.concatenate(sums, axis=1))
                weights = fine_w_ref[2 * LANES * kind : 2 * LANES * (kind + 1), :columns]
                finish(matmul(jnp.concatenate(lhs, axis=0), weights))
        else:
            lower = lanes_of((SLOTS, LANES)) < LANES // 2
            low_sums = lanes_of((8, LANES)) < LANES // 2
            for kind in range(2):
                sums = sum_parts(jnp.where(low_sums, following, now) if kind else now, count)
                weights = coarse_w_ref[2 * LANES * kind : 2 * LANES * (kind + 1), :columns]
                out = None
                for h in range(2):
                    lhs = [
                        jnp.concatenate(
                            [
                                jnp.where(lower, part[t + 1][h], part[t][h]) if kind else part[t][h]
                                for part in (real, imag)
                            ],
                            axis=1,
                        )
                        for t in range(count)
                    ]
                    lhs.append(jnp.concatenate([sums[h], jnp.zeros_like(sums[h])], axis=1))
                    term = matmul(jnp.concatenate(lhs, axis=0), weights)
                    out = term if out is None else out + term
                finish(out)
    return done


def block_transpose(value):
    row = lax.broadcasted_iota(jnp.int32, value.shape, 0) % 4
    block = lax.broadcasted_iota(jnp.int32, value.shape, 1) // WINDOW
    rows = value.shape[0]
    moved = pltpu.roll(value, 2 * WINDOW, 1)
    other = jnp.where(row < 2, pltpu.roll(moved, rows - 2, 0), pltpu.roll(moved, 2, 0))
    value = jnp.where((row // 2) == (block // 2), value, other)
    right = pltpu.roll(pltpu.roll(value, WINDOW, 1), rows - 1, 0)
    left = pltpu.roll(pltpu.roll(value, LANES - WINDOW, 1), 1, 0)
    other = jnp.where(row % 2 == 0, right, left)
    return jnp.where((row % 2) == (block % 2), value, other)


def compute(const_count, *refs):
    pixels_ref, fine_mask_ref, coarse_mask_ref = refs[:3]
    sources = refs[3 : 3 + const_count]
    fine_out_ref, coarse_out_ref = refs[3 + const_count : 5 + const_count]
    main_ref, rim_ref, own_ref, scale_ref = refs[5 + const_count : 9 + const_count]
    held = refs[9 + const_count : 9 + 2 * const_count]
    own_sem, const_sem, send_sem, main_sem, rim_sem = refs[9 + 2 * const_count :]
    sec, strip = lax.axis_index("sec"), lax.axis_index("strip")
    secs, strips = lax.axis_size("sec"), lax.axis_size("strip")
    even, odd = strip % 2 == 0, strip % 2 == 1
    below = strip + 1 < strips
    has_near, has_far = sec + 1 < secs, sec + 2 < secs

    barrier = pltpu.get_barrier_semaphore()

    def greet(condition, device):
        @pl.when(condition)
        def _():
            pl.semaphore_signal(barrier, inc=1, device_id=device, device_id_type=MESH)

    greet(even & has_far, {"sec": sec + 2})
    greet(odd & has_near & below, {"sec": sec + 1, "strip": strip + 1})
    greet(has_near, {"sec": sec + 1})
    greet(below, {"strip": strip + 1})

    own_copy = pltpu.make_async_copy(pixels_ref.at[0], main_ref.at[0], own_sem)
    own_copy.start()
    const_copies = [
        pltpu.make_async_copy(source, target, const_sem.at[index])
        for index, (source, target) in enumerate(zip(sources, held))
    ]
    for copy in const_copies:
        copy.start()

    diagonal = even & (sec >= 1) & (strip >= 1)
    routed = even & (sec >= 2)
    one = lambda condition: jnp.where(condition, 1, 0)
    targets = one(sec >= 1) + one(strip >= 1) + one(diagonal) + one(routed)

    @pl.when(targets >= 1)
    def _():
        pl.semaphore_wait(barrier, targets)

    piece = pixels_ref.shape[2] // CHUNKS

    def remote(flow, source, target, sems, section, device):
        def chunk(c):
            columns = (slice(None), pl.ds(piece * c, piece))
            return pltpu.make_async_remote_copy(
                src_ref=source.at[columns],
                dst_ref=target.at[section].at[columns],
                send_sem=send_sem.at[flow, c],
                recv_sem=sems.at[section, c],
                device_id=device,
                device_id_type=MESH,
            )

        return [chunk(c) for c in range(CHUNKS)]

    own = pixels_ref.at[0]
    above, before = {"strip": strip - 1}, {"sec": sec - 1}
    near_send = remote(0, own, main_ref, main_sem, 1, before)
    rim_send = remote(1, own, rim_ref, rim_sem, 0, above)
    diagonal_send = remote(2, own, rim_ref, rim_sem, 1, {"sec": sec - 1, "strip": strip - 1})
    routed_send = remote(3, own, main_ref, main_sem, 2, {"sec": sec - 2})
    far_relay = remote(4, main_ref.at[1], main_ref, main_sem, 2, before)
    near_rim_relay = remote(5, main_ref.at[1], rim_ref, rim_sem, 1, above)
    far_rim_relay = remote(6, rim_ref.at[1], rim_ref, rim_sem, 2, before)
    far_rim_across = remote(7, main_ref.at[2], rim_ref, rim_sem, 2, above)

    def each(condition, copies, method):
        @pl.when(condition)
        def _():
            for copy in copies:
                getattr(copy, method)()

    each(strip >= 1, rim_send, "start")
    each(diagonal, diagonal_send, "start")
    each(sec >= 1, near_send, "start")
    each(routed, routed_send, "start")

    @pl.when(jnp.logical_not(below))
    def _():
        rim_ref[...] = jnp.zeros_like(rim_ref)

    fine_rows, fine_cols = fine_mask_ref.shape[1:]
    coarse_rows, coarse_cols = coarse_mask_ref.shape[1:]
    fine_groups = fine_rows * fine_cols // 4
    count = fine_groups + coarse_rows * coarse_cols // 4
    fine_w_ref, coarse_w_ref, inverse_ref, last_ref = held[:4]
    first_refs = held[4:]
    inner = inner_rows(pixels_ref.shape[1])
    tiles = pixels_ref.shape[2] // LANES
    bounds = {
        "inner": (0, inner * tiles, 0),
        "outer": (inner * tiles, count, 4 * inner),
    }
    gain = table_gain()

    def spread(mask, cols):
        source = lax.broadcasted_iota(jnp.int32, (cols, cols * WINDOW), 0)
        target = lax.broadcasted_iota(jnp.int32, (cols, cols * WINDOW), 1) // WINDOW
        picks = jnp.where(source == target, 1.0, 0.0).astype(BF16)
        return matmul(mask.astype(F32).astype(BF16), picks)

    fine_mask = spread(fine_mask_ref[0], fine_cols)
    coarse_mask = spread(coarse_mask_ref[0], coarse_cols)
    masks = [
        m[r : r + 1, LANES * t : LANES * (t + 1)]
        for m in (fine_mask, coarse_mask)
        for r in range(m.shape[0])
        for t in range(m.shape[1] // LANES)
    ]

    def squares(out, sums):
        row = rows_of((8, LANES))
        extra = sums * sums * 0.5
        parts = []
        for t in range(tiles):
            block = out[SLOTS * t : SLOTS * (t + 1)]
            block = block * block
            total = jnp.where(row == 0, 0.5 * block[:8], block[:8])
            for r in range(8, SLOTS, 8):
                total = total + block[r : r + 8]
            total = total + jnp.where(row == t, extra, 0.0)
            parts.append(jnp.sum(total, axis=1, keepdims=True))
        return parts

    def members(blocks, coarse):
        if not coarse:
            return [[(kind, t) for kind in range(4)] for t in range(tiles)]
        return [[(p % 2, 2 * g + p // 2) for p in range(4)] for g in range(tiles // 2)]

    def units_of(spectra, part):
        number = (inner if part == "inner" else fine_rows - inner) * 4
        found = [(spectra[at : at + 4], False) for at in range(0, number, 4)]
        return found + [(spectra[at : at + 2], True) for at in range(number, len(spectra), 2)]

    def analyse(section, part):
        start, stop, block = bounds[part]
        if start == stop:
            return
        if part == "inner":
            pixels, rows = main_ref[section], (inner, 0)
        else:
            pixels = jnp.concatenate([main_ref[section], rim_ref[section]], axis=0)
            rows = (fine_rows - inner, coarse_rows)
        first = first_refs[0 if part == "inner" else -1][...]
        columns = LANES if section == 0 else 2 * LANES
        spectra = section_spectra(pixels, first, fine_w_ref, coarse_w_ref, *rows, columns)
        lane = lanes_of((8, LANES)) // WINDOW
        totals = []
        for blocks, coarse in units_of(spectra, part):
            powers = [squares(out[:, :LANES], sums[:, :LANES]) for out, sums in blocks]
            for group in members(blocks, coarse):
                kind, t = group[3]
                total = jnp.broadcast_to(powers[kind][t], (8, LANES))
                for p in range(3):
                    kind, t = group[p]
                    total = jnp.where(lane == p, powers[kind][t], total)
                totals.append(jnp.sum(total, axis=0, keepdims=True))
        total = jnp.concatenate(totals, axis=0)
        scale = 1.0 / jnp.sqrt(total * (2.0 / (float(PATCH) ** 4 * gain * gain)) + 1e-05)
        if section == 0:
            scale_ref[start:stop] = scale
            for index, (out, sums) in enumerate(spectra):
                own_ref[block + index, : SLOTS * tiles] = out[: SLOTS * tiles]
                own_ref[block + index, SLOTS * tiles :] = sums
            return
        correlate(section, part, spectra, scale)

    def correlate(d, part, spectra, other_scale):
        start, stop, block = bounds[part]
        row = rows_of((8, LANES))
        lhs, group_rows, sum_at = [], [], []
        at = 0
        for blocks, coarse in units_of(spectra, part):
            products = []
            for index, (out, sums) in enumerate(blocks):
                own = own_ref[block + index]
                own_rows, own_sums = own[: SLOTS * tiles], own[SLOTS * tiles :]
                body = [(own_rows * tile).astype(BF16) for tile in tiles_of(out[: SLOTS * tiles])]
                tail = [own_sums * tile for tile in tiles_of(sums)]
                products.append((body, tail))
            block += len(blocks)
            groups = members(blocks, coarse)
            pieces = []
            for p in range(4):
                body = [
                    jnp.concatenate([x[SLOTS * t : SLOTS * (t + 1)] for x in products[kind][0]], axis=1)
                    for kind, t in (group[p] for group in groups)
                ]
                tail = products[groups[0][p][0]][1]
                if coarse:
                    tail = [jnp.where(row % 2 == p // 2, x, 0.0) for x in tail]
                body.append(jnp.concatenate([x.astype(BF16) for x in tail], axis=1))
                pieces.append(jnp.concatenate(body, axis=0))
            lhs.append(jnp.concatenate(pieces, axis=1))
            for g in range(len(groups)):
                group_rows.append(at + SLOTS * g)
                base = at + SLOTS * len(groups)
                sum_at.append([base + 2 * g, base + 2 * g + 1] if coarse else [base + g])
            at += SLOTS * len(groups) + 8
        rows = jnp.concatenate([matmul(x, inverse_ref[...]) for x in lhs], axis=0)
        stacked = []
        for r in group_rows:
            piece = rows[r : r + SLOTS]
            stacked.append(jnp.concatenate([piece[:, :LANES], piece[:, LANES:]], axis=0))
        high, low = split_value(jnp.concatenate(stacked, axis=1))
        maps = matmul(last_ref[...], jnp.concatenate([high, low, high], axis=0))
        both = scale_ref[start:stop] * other_scale * (1.0 / (float(PATCH) ** 3 * gain**3))
        for g in range(start, stop):
            at = g - start
            scale = both[at : at + 1] * masks[g]
            value = maps[:, LANES * at : LANES * (at + 1)]
            for r in sum_at[at]:
                value = value + rows[r : r + 1, :LANES]
            value = block_transpose(value * scale)
            if g < fine_groups:
                ref, local_g, cols = fine_out_ref, g, fine_cols
            else:
                ref, local_g, cols = coarse_out_ref, g - fine_groups, coarse_cols
            i, j = divmod(4 * local_g, cols)
            for q in range(WINDOW // 4):
                ref[0, d - 1, i, j : j + 4, LANES * q : LANES * (q + 1)] = value[4 * q : 4 * (q + 1)]

    def clear(d):
        for ref in (fine_out_ref, coarse_out_ref):
            ref[0, d - 1] = jnp.zeros(ref.shape[2:], F32)

    own_copy.wait()
    for copy in const_copies:
        copy.wait()
    analyse(0, "inner")
    @pl.when(has_near)
    def _():
        for c in range(CHUNKS):
            near_send[c].wait_recv()
            pl.when(odd & (sec >= 1))(far_relay[c].start)
            pl.when(odd)(near_rim_relay[c].start)

    each(below, rim_send, "wait_recv")
    analyse(0, "outer")

    @pl.when(has_near)
    def _():
        @pl.when(below)
        def _():
            for c in range(CHUNKS):
                near_rim_relay[c].wait_recv()
                pl.when(odd & (sec >= 1))(far_rim_relay[c].start)

        analyse(1, "inner")
        analyse(1, "outer")

    @pl.when(has_far)
    def _():
        for c in range(CHUNKS):
            far_relay[c].wait_recv()
            pl.when(odd)(far_rim_across[c].start)

    @pl.when(has_far)
    def _():
        analyse(2, "inner")
        each(below, far_rim_relay, "wait_recv")
        analyse(2, "outer")

    pl.when(jnp.logical_not(has_near))(lambda: clear(1))
    pl.when(jnp.logical_not(has_far))(lambda: clear(2))
    each(sec >= 1, near_send, "wait_send")
    each(strip >= 1, rim_send, "wait_send")
    each(diagonal, diagonal_send, "wait_send")
    each(routed, routed_send, "wait_send")
    each(odd & has_near & (sec >= 1), far_relay, "wait_send")
    each(odd & has_near, near_rim_relay, "wait_send")
    each(odd & has_near & below & (sec >= 1), far_rim_relay, "wait_send")
    each(odd & has_far, far_rim_across, "wait_send")


def deliver(fine_ref, coarse_ref, fine_out_ref, coarse_out_ref, sem):
    copies = [
        pltpu.make_async_copy(source.at[0, d], target.at[0, d], sem.at[index, d])
        for index, (source, target) in enumerate(((fine_ref, fine_out_ref), (coarse_ref, coarse_out_ref)))
        for d in range(2)
    ]
    for copy in copies:
        copy.start()
    for copy in copies:
        copy.wait()


def local(sections, mask_fine, mask_coarse):
    strip_rows, width = sections.shape[1:]
    consts = [jnp.asarray(t) for t in tables(strip_rows)]
    fine_rows, fine_cols = mask_fine.shape[1:]
    coarse_rows, coarse_cols = mask_coarse.shape[1:]
    count = (fine_rows * fine_cols + coarse_rows * coarse_cols) // 4
    blocks = 4 * fine_rows + 2 * coarse_rows
    vmem = pl.BlockSpec(memory_space=pltpu.VMEM)
    anywhere = pl.BlockSpec(memory_space=pl.ANY)
    flat = WINDOW * WINDOW
    shapes = (
        jax.ShapeDtypeStruct((1, 2, fine_rows, fine_cols, flat), F32),
        jax.ShapeDtypeStruct((1, 2, coarse_rows, coarse_cols, flat), F32),
    )
    operands = [pltpu.with_memory_space_constraint(t, pltpu.HBM) for t in (sections, mask_fine, mask_coarse, *consts)]
    maps = pl.pallas_call(
        functools.partial(compute, len(consts)),
        out_shape=shapes,
        in_specs=[anywhere, vmem, vmem] + [anywhere] * len(consts),
        out_specs=(vmem, vmem),
        scratch_shapes=[
            pltpu.VMEM((3, strip_rows, width), BF16),
            pltpu.VMEM((3, strip_rows, width), BF16),
            pltpu.VMEM((blocks, SLOTS * (width // LANES) + 8, LANES), F32),
            pltpu.VMEM((count, LANES), F32),
            *[pltpu.VMEM(c.shape, c.dtype) for c in consts],
            pltpu.SemaphoreType.DMA,
            pltpu.SemaphoreType.DMA((len(consts),)),
            pltpu.SemaphoreType.DMA((8, CHUNKS)),
            pltpu.SemaphoreType.DMA((3, CHUNKS)),
            pltpu.SemaphoreType.DMA((3, CHUNKS)),
        ],
        compiler_params=pltpu.CompilerParams(collective_id=0, has_side_effects=True, vmem_limit_bytes=GRANT),
    )(*operands)
    return pl.pallas_call(
        deliver,
        out_shape=shapes,
        in_specs=[vmem, vmem],
        out_specs=(anywhere, anywhere),
        scratch_shapes=[pltpu.SemaphoreType.DMA((2, 2))],
        compiler_params=pltpu.CompilerParams(vmem_limit_bytes=GRANT),
    )(*maps)


def solution(mesh):
    in_specs = (
        P("sec", "strip", "groups"),
        P("sec", "strip", "groups"),
        P("sec", "strip", "groups"),
    )
    out_specs = (P("sec", None, "strip", "groups", None), P("sec", None, "strip", "groups", None))
    return jax.shard_map(local, mesh=mesh, in_specs=in_specs, out_specs=out_specs, check_vma=False)
```

```python
import functools

import jax
import jax.numpy as jnp
import numpy as np
from jax import lax
from jax.experimental import pallas as pl
from jax.experimental.pallas import tpu as pltpu
from jax.sharding import PartitionSpec as P

PATCH = 64
STRIDE = 32
WINDOW = 32
SLOTS = PATCH // 2
CHUNKS = 2
TABLE_SCALE = 1.869
GRANT = 48 * 1024 * 1024
LANES = 128
F32 = jnp.float32
BF16 = jnp.bfloat16
MESH = pl.DeviceIdType.MESH


def trig(phase):
    angle = 2.0 * np.pi / PATCH * np.mod(phase, PATCH)
    return np.round(np.cos(angle), 12), np.round(np.sin(angle), 12)


def split(table):
    high = np.asarray(table, np.float32).astype(BF16)
    low = (np.asarray(table, np.float64) - high.astype(np.float64)).astype(np.float32).astype(BF16)
    return high, low


def block_diagonal(block, count):
    return np.kron(np.eye(count), block)


def rounded(table):
    scaled = np.asarray(table, np.float64) * TABLE_SCALE
    return scaled.astype(np.float32).astype(BF16)


def table_gain():
    c, _ = trig(np.arange(PATCH))
    return float(c @ rounded(c).astype(np.float64) / (c @ c))


def inner_rows(strip_rows):
    return len([i for i in range(strip_rows // STRIDE) if STRIDE * i + PATCH <= strip_rows])


def tables(strip_rows):
    fine_rows = strip_rows // STRIDE
    coarse_rows = strip_rows // (2 * STRIDE)
    inner = inner_rows(strip_rows)
    height = strip_rows + PATCH
    k = np.concatenate([[PATCH // 2], np.arange(1, SLOTS)])[:, None]
    x = np.arange(height)[None, :]
    units, sums = [], []
    for i in range(fine_rows):
        inside = ((x >= STRIDE * i) & (x < STRIDE * i + PATCH)) * 1.0
        c, s = trig(k * (x - STRIDE * i))
        units.append(np.concatenate([c * inside, -s * inside]))
        sums.append(np.repeat(inside, 8, axis=0))
    for i in range(coarse_rows):
        xc = x // 2 - STRIDE * i
        inside = ((xc >= 0) & (xc < PATCH)) * 0.25
        c, s = trig(k * xc)
        units.append(np.concatenate([c * inside, -s * inside]))
        sums.append(np.repeat(inside, 8, axis=0))

    def first(at, rows):
        high, low = split(np.concatenate(units[at] + sums[at], axis=0)[:, :rows])
        return np.concatenate([high, low], axis=1)

    firsts = [first(slice(inner, None), height)]
    if inner:
        firsts.insert(0, first(slice(0, inner), strip_rows))

    lane = np.arange(LANES)
    half, quarter = LANES // 2, LANES // 4
    middle = (lane >= quarter) & (lane < 3 * quarter)
    windows = [
        (lane % half, lane >= half),
        (np.where(middle, lane - quarter, np.where(lane < quarter, lane + quarter, lane - 3 * quarter)), ~middle),
        (lane % half, lane < half),
        (np.where(lane < quarter, lane + quarter, np.where(middle, lane - quarter, lane - 3 * quarter)), middle),
    ]
    freq = np.arange(PATCH)[None, :]

    def weights(y, is_imag):
        c, s = trig(y[:, None] * freq)
        from_real = np.concatenate([c, -s, -s, -c], axis=1)
        from_imag = np.concatenate([s, c, c, -s], axis=1)
        return rounded(np.where(is_imag[:, None], from_imag, from_real))

    fine_w = np.concatenate([np.concatenate([weights(*w)] * 2, axis=0) for w in windows], axis=0)
    both = np.arange(2 * LANES) >= LANES
    coarse_w = np.concatenate(
        [weights(np.concatenate([at // 2] * 2), both) for at in (lane, (lane + half) % LANES)], axis=0
    )

    shift = np.arange(WINDOW) - WINDOW // 2
    c, s = trig((np.arange(LANES) % PATCH)[:, None] * shift[None, :])
    inverse = []
    for p in range(4):
        block = np.zeros((2 * LANES, 2 * LANES))
        block[:LANES, WINDOW * p : WINDOW * (p + 1)] = c
        block[:LANES, LANES + WINDOW * p : LANES + WINDOW * (p + 1)] = s
        block[LANES:, WINDOW * p : WINDOW * (p + 1)] = -s
        block[LANES:, LANES + WINDOW * p : LANES + WINDOW * (p + 1)] = c
        inverse.append(rounded(block))

    weight = np.where(k == PATCH // 2, 1.0, 2.0)
    c, s = trig(shift[:, None] * k.T)
    last_high, last_low = split(np.concatenate([c * weight.T, -s * weight.T], axis=1))
    last = np.concatenate([last_high, last_high, last_low], axis=1)
    return [fine_w, coarse_w, np.concatenate(inverse, axis=0), last, *firsts]


def split_value(value):
    high = value.astype(BF16)
    return high, (value - high.astype(F32)).astype(BF16)


def matmul(a, b):
    return jnp.dot(a, b, preferred_element_type=F32)


def lanes_of(shape):
    return lax.broadcasted_iota(jnp.int32, shape, 1)


def rows_of(shape):
    return lax.broadcasted_iota(jnp.int32, shape, 0)


def tiles_of(value):
    return [value[:, LANES * t : LANES * (t + 1)] for t in range(value.shape[1] // LANES)]


def window(kind, real, turned, real_next, turned_next):
    lane = lanes_of(real.shape)
    half, quarter = LANES // 2, LANES // 4
    if kind == 0:
        return jnp.where(lane < half, real, turned)
    if kind == 1:
        return jnp.where((lane >= quarter) & (lane < 3 * quarter), real, turned)
    if kind == 2:
        return jnp.where(lane < half, turned, real)
    left = jnp.where(lane < quarter, real_next, turned)
    right = jnp.where(lane < 3 * quarter, turned_next, real)
    return jnp.where(lane < half, left, right)


def sum_rows(value):
    row = rows_of((8, LANES))
    tiles = tiles_of(value)
    tiles.append(jnp.zeros_like(tiles[0]))
    count = len(tiles) - 1

    def spread(parts):
        out = parts[count - 1]
        for t in range(count - 1):
            out = jnp.where(row % count == t, parts[t], out)
        return out

    return spread(tiles[:-1]), spread(tiles[1:])


def sum_parts(value, count):
    first = rows_of(value.shape) < count
    high, rest = split_value(value)
    high = high.astype(F32)
    middle = rest.astype(F32)
    low = value - high - middle
    return jnp.where(first, high, low).astype(BF16), jnp.where(first, middle, 0.0).astype(BF16)


def section_spectra(pixels, first, fine_w_ref, coarse_w_ref, fine_rows, coarse_rows, columns):
    rows = matmul(first, jnp.concatenate([pixels, pixels], axis=0))
    units = fine_rows + coarse_rows
    count = rows.shape[1] // LANES
    zero = jnp.zeros((SLOTS, LANES), BF16)
    blank = jnp.zeros((8, LANES), F32)
    done = []

    def finish(out):
        sums = out[SLOTS * count : SLOTS * count + 8]
        sums = sums + pltpu.roll(sums, 4, 0)
        sums = jnp.where(lanes_of(sums.shape) % PATCH == 0, 0.0, sums)
        done.append((out, sums))

    for unit in range(units):
        real = tiles_of(rows[2 * SLOTS * unit : 2 * SLOTS * unit + SLOTS])
        imag = tiles_of(rows[2 * SLOTS * unit + SLOTS : 2 * SLOTS * (unit + 1)])
        if unit < fine_rows:
            imag = [pltpu.roll(tile, LANES // 2, 1) for tile in imag]
        real = [split_value(tile) for tile in real] + [(zero, zero)]
        imag = [split_value(tile) for tile in imag] + [(zero, zero)]
        at = 2 * SLOTS * units + 8 * unit
        now, following = sum_rows(rows[at : at + 8])
        if unit < fine_rows:
            for kind in range(4):
                lhs = [
                    jnp.concatenate(
                        [window(kind, real[t][h], imag[t][h], real[t + 1][h], imag[t + 1][h]) for h in range(2)], axis=1
                    )
                    for t in range(count)
                ]
                sums = sum_parts(window(kind, now, blank, following, blank), count)
                lhs.append(jnp.concatenate(sums, axis=1))
                weights = fine_w_ref[2 * LANES * kind : 2 * LANES * (kind + 1), :columns]
                finish(matmul(jnp.concatenate(lhs, axis=0), weights))
        else:
            lower = lanes_of((SLOTS, LANES)) < LANES // 2
            low_sums = lanes_of((8, LANES)) < LANES // 2
            for kind in range(2):
                sums = sum_parts(jnp.where(low_sums, following, now) if kind else now, count)
                weights = coarse_w_ref[2 * LANES * kind : 2 * LANES * (kind + 1), :columns]
                out = None
                for h in range(2):
                    lhs = [
                        jnp.concatenate(
                            [
                                jnp.where(lower, part[t + 1][h], part[t][h]) if kind else part[t][h]
                                for part in (real, imag)
                            ],
                            axis=1,
                        )
                        for t in range(count)
                    ]
                    lhs.append(jnp.concatenate([sums[h], jnp.zeros_like(sums[h])], axis=1))
                    term = matmul(jnp.concatenate(lhs, axis=0), weights)
                    out = term if out is None else out + term
                finish(out)
    return done


def block_transpose(value):
    row = lax.broadcasted_iota(jnp.int32, value.shape, 0) % 4
    block = lax.broadcasted_iota(jnp.int32, value.shape, 1) // WINDOW
    rows = value.shape[0]
    moved = pltpu.roll(value, 2 * WINDOW, 1)
    other = jnp.where(row < 2, pltpu.roll(moved, rows - 2, 0), pltpu.roll(moved, 2, 0))
    value = jnp.where((row // 2) == (block // 2), value, other)
    right = pltpu.roll(pltpu.roll(value, WINDOW, 1), rows - 1, 0)
    left = pltpu.roll(pltpu.roll(value, LANES - WINDOW, 1), 1, 0)
    other = jnp.where(row % 2 == 0, right, left)
    return jnp.where((row % 2) == (block % 2), value, other)


def consts_order(const_count):
    return (4, 0, *range(5, const_count), 1, 2, 3)


def compute(const_count, *refs):
    pixels_ref, fine_source_ref, coarse_source_ref = refs[:3]
    sources = refs[3 : 3 + const_count]
    fine_out_ref, coarse_out_ref = refs[3 + const_count : 5 + const_count]
    main_ref, rim_ref, own_ref, scale_ref, fine_mask_ref, coarse_mask_ref = refs[5 + const_count : 11 + const_count]
    held = refs[11 + const_count : 11 + 2 * const_count]
    own_sem, mask_sem, const_sem, send_sem, main_sem, rim_sem = refs[11 + 2 * const_count :]
    sec, strip = lax.axis_index("sec"), lax.axis_index("strip")
    secs, strips = lax.axis_size("sec"), lax.axis_size("strip")
    even, odd = strip % 2 == 0, strip % 2 == 1
    below = strip + 1 < strips
    has_near, has_far = sec + 1 < secs, sec + 2 < secs

    barrier = pltpu.get_barrier_semaphore()

    def greet(condition, device):
        @pl.when(condition)
        def _():
            pl.semaphore_signal(barrier, inc=1, device_id=device, device_id_type=MESH)

    greet(even & has_far, {"sec": sec + 2})
    greet(odd & has_near & below, {"sec": sec + 1, "strip": strip + 1})
    greet(has_near, {"sec": sec + 1})
    greet(below, {"strip": strip + 1})

    own_copy = pltpu.make_async_copy(pixels_ref.at[0], main_ref.at[0], own_sem)
    own_copy.start()
    const_copies = [
        pltpu.make_async_copy(source, target, const_sem.at[index])
        for index, (source, target) in enumerate(zip(sources, held))
    ]
    for index in consts_order(const_count):
        const_copies[index].start()
    mask_copies = [
        pltpu.make_async_copy(source, target, mask_sem.at[index])
        for index, (source, target) in enumerate(
            ((fine_source_ref, fine_mask_ref), (coarse_source_ref, coarse_mask_ref))
        )
    ]
    for copy in mask_copies:
        copy.start()

    diagonal = even & (sec >= 1) & (strip >= 1)
    routed = even & (sec >= 2)
    one = lambda condition: jnp.where(condition, 1, 0)
    targets = one(sec >= 1) + one(strip >= 1) + one(diagonal) + one(routed)

    @pl.when(targets >= 1)
    def _():
        pl.semaphore_wait(barrier, targets)

    piece = pixels_ref.shape[2] // CHUNKS

    def remote(flow, source, target, sems, section, device):
        def chunk(c):
            columns = (slice(None), pl.ds(piece * c, piece))
            return pltpu.make_async_remote_copy(
                src_ref=source.at[columns],
                dst_ref=target.at[section].at[columns],
                send_sem=send_sem.at[flow, c],
                recv_sem=sems.at[section, c],
                device_id=device,
                device_id_type=MESH,
            )

        return [chunk(c) for c in range(CHUNKS)]

    own = pixels_ref.at[0]
    above, before = {"strip": strip - 1}, {"sec": sec - 1}
    near_send = remote(0, own, main_ref, main_sem, 1, before)
    rim_send = remote(1, own, rim_ref, rim_sem, 0, above)
    diagonal_send = remote(2, own, rim_ref, rim_sem, 1, {"sec": sec - 1, "strip": strip - 1})
    routed_send = remote(3, own, main_ref, main_sem, 2, {"sec": sec - 2})
    far_relay = remote(4, main_ref.at[1], main_ref, main_sem, 2, before)
    near_rim_relay = remote(5, main_ref.at[1], rim_ref, rim_sem, 1, above)
    far_rim_relay = remote(6, rim_ref.at[1], rim_ref, rim_sem, 2, before)
    far_rim_across = remote(7, main_ref.at[2], rim_ref, rim_sem, 2, above)

    def each(condition, copies, method):
        @pl.when(condition)
        def _():
            for copy in copies:
                getattr(copy, method)()

    each(strip >= 1, rim_send, "start")
    each(diagonal, diagonal_send, "start")
    each(sec >= 1, near_send, "start")
    each(routed, routed_send, "start")

    @pl.when(jnp.logical_not(below))
    def _():
        rim_ref[...] = jnp.zeros_like(rim_ref)

    fine_rows, fine_cols = fine_mask_ref.shape[1:]
    coarse_rows, coarse_cols = coarse_mask_ref.shape[1:]
    fine_groups = fine_rows * fine_cols // 4
    count = fine_groups + coarse_rows * coarse_cols // 4
    fine_w_ref, coarse_w_ref, inverse_ref, last_ref = held[:4]
    first_refs = held[4:]
    inner = inner_rows(pixels_ref.shape[1])
    tiles = pixels_ref.shape[2] // LANES
    bounds = {
        "inner": (0, inner * tiles, 0),
        "outer": (inner * tiles, count, 4 * inner),
    }
    gain = table_gain()

    def spread(mask, cols):
        source = lax.broadcasted_iota(jnp.int32, (cols, cols * WINDOW), 0)
        target = lax.broadcasted_iota(jnp.int32, (cols, cols * WINDOW), 1) // WINDOW
        picks = jnp.where(source == target, 1.0, 0.0).astype(BF16)
        return matmul(mask.astype(F32).astype(BF16), picks)

    def mask_rows():
        fine_mask = spread(fine_mask_ref[0], fine_cols)
        coarse_mask = spread(coarse_mask_ref[0], coarse_cols)
        return [
            m[r : r + 1, LANES * t : LANES * (t + 1)]
            for m in (fine_mask, coarse_mask)
            for r in range(m.shape[0])
            for t in range(m.shape[1] // LANES)
        ]

    def squares(out, sums):
        row = rows_of((8, LANES))
        extra = sums * sums * 0.5
        parts = []
        for t in range(tiles):
            block = out[SLOTS * t : SLOTS * (t + 1)]
            block = block * block
            total = jnp.where(row == 0, 0.5 * block[:8], block[:8])
            for r in range(8, SLOTS, 8):
                total = total + block[r : r + 8]
            total = total + jnp.where(row == t, extra, 0.0)
            parts.append(jnp.sum(total, axis=1, keepdims=True))
        return parts

    def members(blocks, coarse):
        if not coarse:
            return [[(kind, t) for kind in range(4)] for t in range(tiles)]
        return [[(p % 2, 2 * g + p // 2) for p in range(4)] for g in range(tiles // 2)]

    def units_of(spectra, part):
        number = (inner if part == "inner" else fine_rows - inner) * 4
        found = [(spectra[at : at + 4], False) for at in range(0, number, 4)]
        return found + [(spectra[at : at + 2], True) for at in range(number, len(spectra), 2)]

    def analyse(section, part):
        start, stop, block = bounds[part]
        if start == stop:
            return
        if part == "inner":
            pixels, rows = main_ref[section], (inner, 0)
        else:
            pixels = jnp.concatenate([main_ref[section], rim_ref[section]], axis=0)
            rows = (fine_rows - inner, coarse_rows)
        first = first_refs[0 if part == "inner" else -1][...]
        columns = LANES if section == 0 else 2 * LANES
        spectra = section_spectra(pixels, first, fine_w_ref, coarse_w_ref, *rows, columns)
        lane = lanes_of((8, LANES)) // WINDOW
        totals = []
        for blocks, coarse in units_of(spectra, part):
            powers = [squares(out[:, :LANES], sums[:, :LANES]) for out, sums in blocks]
            for group in members(blocks, coarse):
                kind, t = group[3]
                total = jnp.broadcast_to(powers[kind][t], (8, LANES))
                for p in range(3):
                    kind, t = group[p]
                    total = jnp.where(lane == p, powers[kind][t], total)
                totals.append(jnp.sum(total, axis=0, keepdims=True))
        total = jnp.concatenate(totals, axis=0)
        scale = 1.0 / jnp.sqrt(total * (2.0 / (float(PATCH) ** 4 * gain * gain)) + 1e-05)
        if section == 0:
            scale_ref[start:stop] = scale
            for index, (out, sums) in enumerate(spectra):
                own_ref[block + index, : SLOTS * tiles] = out[: SLOTS * tiles]
                own_ref[block + index, SLOTS * tiles :] = sums
            return
        correlate(section, part, spectra, scale)

    def correlate(d, part, spectra, other_scale):
        start, stop, block = bounds[part]
        row = rows_of((8, LANES))
        lhs, group_rows, sum_at = [], [], []
        at = 0
        for blocks, coarse in units_of(spectra, part):
            products = []
            for index, (out, sums) in enumerate(blocks):
                own = own_ref[block + index]
                own_rows, own_sums = own[: SLOTS * tiles], own[SLOTS * tiles :]
                body = [(own_rows * tile).astype(BF16) for tile in tiles_of(out[: SLOTS * tiles])]
                tail = [own_sums * tile for tile in tiles_of(sums)]
                products.append((body, tail))
            block += len(blocks)
            groups = members(blocks, coarse)
            pieces = []
            for p in range(4):
                body = [
                    jnp.concatenate([x[SLOTS * t : SLOTS * (t + 1)] for x in products[kind][0]], axis=1)
                    for kind, t in (group[p] for group in groups)
                ]
                tail = products[groups[0][p][0]][1]
                if coarse:
                    tail = [jnp.where(row % 2 == p // 2, x, 0.0) for x in tail]
                body.append(jnp.concatenate([x.astype(BF16) for x in tail], axis=1))
                pieces.append(jnp.concatenate(body, axis=0))
            lhs.append(jnp.concatenate(pieces, axis=1))
            for g in range(len(groups)):
                group_rows.append(at + SLOTS * g)
                base = at + SLOTS * len(groups)
                sum_at.append([base + 2 * g, base + 2 * g + 1] if coarse else [base + g])
            at += SLOTS * len(groups) + 8
        rows = jnp.concatenate([matmul(x, inverse_ref[...]) for x in lhs], axis=0)
        stacked = []
        for r in group_rows:
            piece = rows[r : r + SLOTS]
            stacked.append(jnp.concatenate([piece[:, :LANES], piece[:, LANES:]], axis=0))
        high, low = split_value(jnp.concatenate(stacked, axis=1))
        maps = matmul(last_ref[...], jnp.concatenate([high, low, high], axis=0))
        both = scale_ref[start:stop] * other_scale * (1.0 / (float(PATCH) ** 3 * gain**3))
        for g in range(start, stop):
            at = g - start
            scale = both[at : at + 1] * masks[g]
            value = maps[:, LANES * at : LANES * (at + 1)]
            for r in sum_at[at]:
                value = value + rows[r : r + 1, :LANES]
            value = block_transpose(value * scale)
            if g < fine_groups:
                ref, local_g, cols = fine_out_ref, g, fine_cols
            else:
                ref, local_g, cols = coarse_out_ref, g - fine_groups, coarse_cols
            i, j = divmod(4 * local_g, cols)
            for q in range(WINDOW // 4):
                ref[0, d - 1, i, j : j + 4, LANES * q : LANES * (q + 1)] = value[4 * q : 4 * (q + 1)]

    def clear(d):
        for ref in (fine_out_ref, coarse_out_ref):
            ref[0, d - 1] = jnp.zeros(ref.shape[2:], F32)

    own_copy.wait()
    for index in consts_order(const_count)[:2]:
        const_copies[index].wait()
    analyse(0, "inner")
    for index in consts_order(const_count)[2:]:
        const_copies[index].wait()
    for copy in mask_copies:
        copy.wait()
    masks = mask_rows()
    @pl.when(has_near)
    def _():
        for c in range(CHUNKS):
            near_send[c].wait_recv()
            pl.when(odd & (sec >= 1))(far_relay[c].start)
            pl.when(odd)(near_rim_relay[c].start)

    each(below, rim_send, "wait_recv")
    analyse(0, "outer")

    @pl.when(has_near)
    def _():
        @pl.when(below)
        def _():
            for c in range(CHUNKS):
                near_rim_relay[c].wait_recv()
                pl.when(odd & (sec >= 1))(far_rim_relay[c].start)

        analyse(1, "inner")
        analyse(1, "outer")

    @pl.when(has_far)
    def _():
        for c in range(CHUNKS):
            far_relay[c].wait_recv()
            pl.when(odd)(far_rim_across[c].start)

    @pl.when(has_far)
    def _():
        analyse(2, "inner")
        each(below, far_rim_relay, "wait_recv")
        analyse(2, "outer")

    pl.when(jnp.logical_not(has_near))(lambda: clear(1))
    pl.when(jnp.logical_not(has_far))(lambda: clear(2))
    each(sec >= 1, near_send, "wait_send")
    each(strip >= 1, rim_send, "wait_send")
    each(diagonal, diagonal_send, "wait_send")
    each(routed, routed_send, "wait_send")
    each(odd & has_near & (sec >= 1), far_relay, "wait_send")
    each(odd & has_near, near_rim_relay, "wait_send")
    each(odd & has_near & below & (sec >= 1), far_rim_relay, "wait_send")
    each(odd & has_far, far_rim_across, "wait_send")


def deliver(fine_ref, coarse_ref, fine_out_ref, coarse_out_ref, sem):
    copies = [
        pltpu.make_async_copy(source.at[0, d], target.at[0, d], sem.at[index, d])
        for index, (source, target) in enumerate(((fine_ref, fine_out_ref), (coarse_ref, coarse_out_ref)))
        for d in range(2)
    ]
    for copy in copies:
        copy.start()
    for copy in copies:
        copy.wait()


def local(sections, mask_fine, mask_coarse):
    strip_rows, width = sections.shape[1:]
    consts = [jnp.asarray(t) for t in tables(strip_rows)]
    fine_rows, fine_cols = mask_fine.shape[1:]
    coarse_rows, coarse_cols = mask_coarse.shape[1:]
    count = (fine_rows * fine_cols + coarse_rows * coarse_cols) // 4
    blocks = 4 * fine_rows + 2 * coarse_rows
    vmem = pl.BlockSpec(memory_space=pltpu.VMEM)
    anywhere = pl.BlockSpec(memory_space=pl.ANY)
    flat = WINDOW * WINDOW
    shapes = (
        jax.ShapeDtypeStruct((1, 2, fine_rows, fine_cols, flat), F32),
        jax.ShapeDtypeStruct((1, 2, coarse_rows, coarse_cols, flat), F32),
    )
    operands = [pltpu.with_memory_space_constraint(t, pltpu.HBM) for t in (sections, mask_fine, mask_coarse, *consts)]
    maps = pl.pallas_call(
        functools.partial(compute, len(consts)),
        out_shape=shapes,
        in_specs=[anywhere] * (3 + len(consts)),
        out_specs=(vmem, vmem),
        scratch_shapes=[
            pltpu.VMEM((3, strip_rows, width), BF16),
            pltpu.VMEM((3, strip_rows, width), BF16),
            pltpu.VMEM((blocks, SLOTS * (width // LANES) + 8, LANES), F32),
            pltpu.VMEM((count, LANES), F32),
            pltpu.VMEM(mask_fine.shape, mask_fine.dtype),
            pltpu.VMEM(mask_coarse.shape, mask_coarse.dtype),
            *[pltpu.VMEM(c.shape, c.dtype) for c in consts],
            pltpu.SemaphoreType.DMA,
            pltpu.SemaphoreType.DMA((2,)),
            pltpu.SemaphoreType.DMA((len(consts),)),
            pltpu.SemaphoreType.DMA((8, CHUNKS)),
            pltpu.SemaphoreType.DMA((3, CHUNKS)),
            pltpu.SemaphoreType.DMA((3, CHUNKS)),
        ],
        compiler_params=pltpu.CompilerParams(collective_id=0, has_side_effects=True, vmem_limit_bytes=GRANT),
    )(*operands)
    return pl.pallas_call(
        deliver,
        out_shape=shapes,
        in_specs=[vmem, vmem],
        out_specs=(anywhere, anywhere),
        scratch_shapes=[pltpu.SemaphoreType.DMA((2, 2))],
        compiler_params=pltpu.CompilerParams(vmem_limit_bytes=GRANT),
    )(*maps)


def solution(mesh):
    in_specs = (
        P("sec", "strip", "groups"),
        P("sec", "strip", "groups"),
        P("sec", "strip", "groups"),
    )
    out_specs = (P("sec", None, "strip", "groups", None), P("sec", None, "strip", "groups", None))
    return jax.shard_map(local, mesh=mesh, in_specs=in_specs, out_specs=out_specs, check_vma=False)
```

```python
import functools

import jax
import jax.numpy as jnp
import numpy as np
from jax import lax
from jax.experimental import pallas as pl
from jax.experimental.pallas import tpu as pltpu
from jax.sharding import PartitionSpec as P

PATCH = 64
STRIDE = 32
WINDOW = 32
SLOTS = PATCH // 2
CHUNKS = 2
TABLE_SCALE = 1.869
GRANT = 48 * 1024 * 1024
LANES = 128
F32 = jnp.float32
BF16 = jnp.bfloat16
MESH = pl.DeviceIdType.MESH


def trig(phase):
    angle = 2.0 * np.pi / PATCH * np.mod(phase, PATCH)
    return np.round(np.cos(angle), 12), np.round(np.sin(angle), 12)


def split(table):
    high = np.asarray(table, np.float32).astype(BF16)
    low = (np.asarray(table, np.float64) - high.astype(np.float64)).astype(np.float32).astype(BF16)
    return high, low


def block_diagonal(block, count):
    return np.kron(np.eye(count), block)


def rounded(table):
    scaled = np.asarray(table, np.float64) * TABLE_SCALE
    return scaled.astype(np.float32).astype(BF16)


def table_gain():
    c, _ = trig(np.arange(PATCH))
    return float(c @ rounded(c).astype(np.float64) / (c @ c))


def inner_rows(strip_rows):
    return len([i for i in range(strip_rows // STRIDE) if STRIDE * i + PATCH <= strip_rows])


def tables(strip_rows):
    fine_rows = strip_rows // STRIDE
    coarse_rows = strip_rows // (2 * STRIDE)
    inner = inner_rows(strip_rows)
    height = strip_rows + PATCH
    k = np.concatenate([[PATCH // 2], np.arange(1, SLOTS)])[:, None]
    x = np.arange(height)[None, :]
    units, sums = [], []
    for i in range(fine_rows):
        inside = ((x >= STRIDE * i) & (x < STRIDE * i + PATCH)) * 1.0
        c, s = trig(k * (x - STRIDE * i))
        units.append(np.concatenate([c * inside, -s * inside]))
        sums.append(np.repeat(inside, 8, axis=0))
    for i in range(coarse_rows):
        xc = x // 2 - STRIDE * i
        inside = ((xc >= 0) & (xc < PATCH)) * 0.25
        c, s = trig(k * xc)
        units.append(np.concatenate([c * inside, -s * inside]))
        sums.append(np.repeat(inside, 8, axis=0))

    def first(at, rows):
        high, low = split(np.concatenate(units[at] + sums[at], axis=0)[:, :rows])
        return np.concatenate([high, low], axis=1)

    firsts = [first(slice(inner, None), height)]
    if inner:
        firsts.insert(0, first(slice(0, inner), strip_rows))

    lane = np.arange(LANES)
    half, quarter = LANES // 2, LANES // 4
    middle = (lane >= quarter) & (lane < 3 * quarter)
    windows = [
        (lane % half, lane >= half),
        (np.where(middle, lane - quarter, np.where(lane < quarter, lane + quarter, lane - 3 * quarter)), ~middle),
        (lane % half, lane < half),
        (np.where(lane < quarter, lane + quarter, np.where(middle, lane - quarter, lane - 3 * quarter)), middle),
    ]
    freq = np.arange(PATCH)[None, :]

    def weights(y, is_imag):
        c, s = trig(y[:, None] * freq)
        from_real = np.concatenate([c, -s, -s, -c], axis=1)
        from_imag = np.concatenate([s, c, c, -s], axis=1)
        return rounded(np.where(is_imag[:, None], from_imag, from_real))

    fine_w = np.concatenate([np.concatenate([weights(*w)] * 2, axis=0) for w in windows], axis=0)
    both = np.arange(2 * LANES) >= LANES
    coarse_w = np.concatenate(
        [weights(np.concatenate([at // 2] * 2), both) for at in (lane, (lane + half) % LANES)], axis=0
    )

    shift = np.arange(WINDOW) - WINDOW // 2
    c, s = trig((np.arange(LANES) % PATCH)[:, None] * shift[None, :])
    inverse = []
    for p in range(4):
        block = np.zeros((2 * LANES, 2 * LANES))
        block[:LANES, WINDOW * p : WINDOW * (p + 1)] = c
        block[:LANES, LANES + WINDOW * p : LANES + WINDOW * (p + 1)] = s
        block[LANES:, WINDOW * p : WINDOW * (p + 1)] = -s
        block[LANES:, LANES + WINDOW * p : LANES + WINDOW * (p + 1)] = c
        inverse.append(rounded(block))

    weight = np.where(k == PATCH // 2, 1.0, 2.0)
    c, s = trig(shift[:, None] * k.T)
    last_high, last_low = split(np.concatenate([c * weight.T, -s * weight.T], axis=1))
    last = np.concatenate([last_high, last_high, last_low], axis=1)
    return [fine_w, coarse_w, np.concatenate(inverse, axis=0), last, *firsts]


def split_value(value):
    high = value.astype(BF16)
    return high, (value - high.astype(F32)).astype(BF16)


def matmul(a, b):
    return jnp.dot(a, b, preferred_element_type=F32)


def lanes_of(shape):
    return lax.broadcasted_iota(jnp.int32, shape, 1)


def rows_of(shape):
    return lax.broadcasted_iota(jnp.int32, shape, 0)


def tiles_of(value):
    return [value[:, LANES * t : LANES * (t + 1)] for t in range(value.shape[1] // LANES)]


def window(kind, real, turned, real_next, turned_next):
    lane = lanes_of(real.shape)
    half, quarter = LANES // 2, LANES // 4
    if kind == 0:
        return jnp.where(lane < half, real, turned)
    if kind == 1:
        return jnp.where((lane >= quarter) & (lane < 3 * quarter), real, turned)
    if kind == 2:
        return jnp.where(lane < half, turned, real)
    left = jnp.where(lane < quarter, real_next, turned)
    right = jnp.where(lane < 3 * quarter, turned_next, real)
    return jnp.where(lane < half, left, right)


def sum_rows(value):
    row = rows_of((8, LANES))
    tiles = tiles_of(value)
    tiles.append(jnp.zeros_like(tiles[0]))
    count = len(tiles) - 1

    def spread(parts):
        out = parts[count - 1]
        for t in range(count - 1):
            out = jnp.where(row % count == t, parts[t], out)
        return out

    return spread(tiles[:-1]), spread(tiles[1:])


def sum_parts(value, count):
    first = rows_of(value.shape) < count
    high, rest = split_value(value)
    high = high.astype(F32)
    middle = rest.astype(F32)
    low = value - high - middle
    return jnp.where(first, high, low).astype(BF16), jnp.where(first, middle, 0.0).astype(BF16)


def section_spectra(pixels, first, fine_w_ref, coarse_w_ref, fine_rows, coarse_rows, columns):
    rows = matmul(first, jnp.concatenate([pixels, pixels], axis=0))
    units = fine_rows + coarse_rows
    count = rows.shape[1] // LANES
    zero = jnp.zeros((SLOTS, LANES), BF16)
    blank = jnp.zeros((8, LANES), F32)
    done = []

    def finish(out):
        sums = out[SLOTS * count : SLOTS * count + 8]
        sums = sums + pltpu.roll(sums, 4, 0)
        sums = jnp.where(lanes_of(sums.shape) % PATCH == 0, 0.0, sums)
        done.append((out, sums))

    for unit in range(units):
        real = tiles_of(rows[2 * SLOTS * unit : 2 * SLOTS * unit + SLOTS])
        imag = tiles_of(rows[2 * SLOTS * unit + SLOTS : 2 * SLOTS * (unit + 1)])
        if unit < fine_rows:
            imag = [pltpu.roll(tile, LANES // 2, 1) for tile in imag]
        real = [split_value(tile) for tile in real] + [(zero, zero)]
        imag = [split_value(tile) for tile in imag] + [(zero, zero)]
        at = 2 * SLOTS * units + 8 * unit
        now, following = sum_rows(rows[at : at + 8])
        if unit < fine_rows:
            for kind in range(4):
                lhs = [
                    jnp.concatenate(
                        [window(kind, real[t][h], imag[t][h], real[t + 1][h], imag[t + 1][h]) for h in range(2)], axis=1
                    )
                    for t in range(count)
                ]
                sums = sum_parts(window(kind, now, blank, following, blank), count)
                lhs.append(jnp.concatenate(sums, axis=1))
                weights = fine_w_ref[2 * LANES * kind : 2 * LANES * (kind + 1), :columns]
                finish(matmul(jnp.concatenate(lhs, axis=0), weights))
        else:
            lower = lanes_of((SLOTS, LANES)) < LANES // 2
            low_sums = lanes_of((8, LANES)) < LANES // 2
            for kind in range(2):
                sums = sum_parts(jnp.where(low_sums, following, now) if kind else now, count)
                weights = coarse_w_ref[2 * LANES * kind : 2 * LANES * (kind + 1), :columns]
                out = None
                for h in range(2):
                    lhs = [
                        jnp.concatenate(
                            [
                                jnp.where(lower, part[t + 1][h], part[t][h]) if kind else part[t][h]
                                for part in (real, imag)
                            ],
                            axis=1,
                        )
                        for t in range(count)
                    ]
                    lhs.append(jnp.concatenate([sums[h], jnp.zeros_like(sums[h])], axis=1))
                    term = matmul(jnp.concatenate(lhs, axis=0), weights)
                    out = term if out is None else out + term
                finish(out)
    return done


def block_transpose(value):
    row = lax.broadcasted_iota(jnp.int32, value.shape, 0) % 4
    block = lax.broadcasted_iota(jnp.int32, value.shape, 1) // WINDOW
    rows = value.shape[0]
    moved = pltpu.roll(value, 2 * WINDOW, 1)
    other = jnp.where(row < 2, pltpu.roll(moved, rows - 2, 0), pltpu.roll(moved, 2, 0))
    value = jnp.where((row // 2) == (block // 2), value, other)
    right = pltpu.roll(pltpu.roll(value, WINDOW, 1), rows - 1, 0)
    left = pltpu.roll(pltpu.roll(value, LANES - WINDOW, 1), 1, 0)
    other = jnp.where(row % 2 == 0, right, left)
    return jnp.where((row % 2) == (block % 2), value, other)


def consts_order(const_count):
    return (4, 0, *range(5, const_count), 1, 2, 3)


def compute(const_count, *refs):
    pixels_ref, fine_source_ref, coarse_source_ref = refs[:3]
    sources = refs[3 : 3 + const_count]
    fine_out_ref, coarse_out_ref = refs[3 + const_count : 5 + const_count]
    main_ref, rim_ref, own_ref, scale_ref, fine_mask_ref, coarse_mask_ref = refs[5 + const_count : 11 + const_count]
    held = refs[11 + const_count : 11 + 2 * const_count]
    own_sem, mask_sem, const_sem, send_sem, main_sem, rim_sem = refs[11 + 2 * const_count :]
    sec, strip = lax.axis_index("sec"), lax.axis_index("strip")
    secs, strips = lax.axis_size("sec"), lax.axis_size("strip")
    even, odd = strip % 2 == 0, strip % 2 == 1
    below = strip + 1 < strips
    has_near, has_far = sec + 1 < secs, sec + 2 < secs

    barrier = pltpu.get_barrier_semaphore()

    def greet(condition, device):
        @pl.when(condition)
        def _():
            pl.semaphore_signal(barrier, inc=1, device_id=device, device_id_type=MESH)

    greet(has_near, {"sec": sec + 1})
    greet(even & has_far, {"sec": sec + 2})
    greet(odd & has_near & below, {"sec": sec + 1, "strip": strip + 1})
    greet(below, {"strip": strip + 1})

    own_copy = pltpu.make_async_copy(pixels_ref.at[0], main_ref.at[0], own_sem)
    own_copy.start()
    const_copies = [
        pltpu.make_async_copy(source, target, const_sem.at[index])
        for index, (source, target) in enumerate(zip(sources, held))
    ]
    for index in consts_order(const_count):
        const_copies[index].start()
    mask_copies = [
        pltpu.make_async_copy(source, target, mask_sem.at[index])
        for index, (source, target) in enumerate(
            ((fine_source_ref, fine_mask_ref), (coarse_source_ref, coarse_mask_ref))
        )
    ]
    for copy in mask_copies:
        copy.start()

    diagonal = even & (sec >= 1) & (strip >= 1)
    routed = even & (sec >= 2)
    one = lambda condition: jnp.where(condition, 1, 0)
    targets = one(sec >= 1) + one(strip >= 1) + one(diagonal) + one(routed)

    @pl.when(targets >= 1)
    def _():
        pl.semaphore_wait(barrier, targets)

    piece = pixels_ref.shape[2] // CHUNKS

    def remote(flow, source, target, sems, section, device):
        def chunk(c):
            columns = (slice(None), pl.ds(piece * c, piece))
            return pltpu.make_async_remote_copy(
                src_ref=source.at[columns],
                dst_ref=target.at[section].at[columns],
                send_sem=send_sem.at[flow, c],
                recv_sem=sems.at[section, c],
                device_id=device,
                device_id_type=MESH,
            )

        return [chunk(c) for c in range(CHUNKS)]

    own = pixels_ref.at[0]
    above, before = {"strip": strip - 1}, {"sec": sec - 1}
    near_send = remote(0, own, main_ref, main_sem, 1, before)
    rim_send = remote(1, own, rim_ref, rim_sem, 0, above)
    diagonal_send = remote(2, own, rim_ref, rim_sem, 1, {"sec": sec - 1, "strip": strip - 1})
    routed_send = remote(3, own, main_ref, main_sem, 2, {"sec": sec - 2})
    far_relay = remote(4, main_ref.at[1], main_ref, main_sem, 2, before)
    near_rim_relay = remote(5, main_ref.at[1], rim_ref, rim_sem, 1, above)
    far_rim_relay = remote(6, rim_ref.at[1], rim_ref, rim_sem, 2, before)
    far_rim_across = remote(7, main_ref.at[2], rim_ref, rim_sem, 2, above)

    def each(condition, copies, method):
        @pl.when(condition)
        def _():
            for copy in copies:
                getattr(copy, method)()

    each(odd & (sec >= 1), near_send, "start")
    each(strip >= 1, rim_send, "start")
    each(diagonal, diagonal_send, "start")
    each(even & (sec >= 1), near_send, "start")
    each(routed, routed_send, "start")

    @pl.when(jnp.logical_not(below))
    def _():
        rim_ref[...] = jnp.zeros_like(rim_ref)

    fine_rows, fine_cols = fine_mask_ref.shape[1:]
    coarse_rows, coarse_cols = coarse_mask_ref.shape[1:]
    fine_groups = fine_rows * fine_cols // 4
    count = fine_groups + coarse_rows * coarse_cols // 4
    fine_w_ref, coarse_w_ref, inverse_ref, last_ref = held[:4]
    first_refs = held[4:]
    inner = inner_rows(pixels_ref.shape[1])
    tiles = pixels_ref.shape[2] // LANES
    bounds = {
        "inner": (0, inner * tiles, 0),
        "outer": (inner * tiles, count, 4 * inner),
    }
    gain = table_gain()

    def spread(mask, cols):
        source = lax.broadcasted_iota(jnp.int32, (cols, cols * WINDOW), 0)
        target = lax.broadcasted_iota(jnp.int32, (cols, cols * WINDOW), 1) // WINDOW
        picks = jnp.where(source == target, 1.0, 0.0).astype(BF16)
        return matmul(mask.astype(F32).astype(BF16), picks)

    def mask_rows():
        fine_mask = spread(fine_mask_ref[0], fine_cols)
        coarse_mask = spread(coarse_mask_ref[0], coarse_cols)
        return [
            m[r : r + 1, LANES * t : LANES * (t + 1)]
            for m in (fine_mask, coarse_mask)
            for r in range(m.shape[0])
            for t in range(m.shape[1] // LANES)
        ]

    def squares(out, sums):
        row = rows_of((8, LANES))
        extra = sums * sums * 0.5
        parts = []
        for t in range(tiles):
            block = out[SLOTS * t : SLOTS * (t + 1)]
            block = block * block
            total = jnp.where(row == 0, 0.5 * block[:8], block[:8])
            for r in range(8, SLOTS, 8):
                total = total + block[r : r + 8]
            total = total + jnp.where(row == t, extra, 0.0)
            parts.append(jnp.sum(total, axis=1, keepdims=True))
        return parts

    def members(blocks, coarse):
        if not coarse:
            return [[(kind, t) for kind in range(4)] for t in range(tiles)]
        return [[(p % 2, 2 * g + p // 2) for p in range(4)] for g in range(tiles // 2)]

    def units_of(spectra, part):
        number = (inner if part == "inner" else fine_rows - inner) * 4
        found = [(spectra[at : at + 4], False) for at in range(0, number, 4)]
        return found + [(spectra[at : at + 2], True) for at in range(number, len(spectra), 2)]

    def analyse(section, part):
        start, stop, block = bounds[part]
        if start == stop:
            return
        if part == "inner":
            pixels, rows = main_ref[section], (inner, 0)
        else:
            pixels = jnp.concatenate([main_ref[section], rim_ref[section]], axis=0)
            rows = (fine_rows - inner, coarse_rows)
        first = first_refs[0 if part == "inner" else -1][...]
        columns = LANES if section == 0 else 2 * LANES
        spectra = section_spectra(pixels, first, fine_w_ref, coarse_w_ref, *rows, columns)
        lane = lanes_of((8, LANES)) // WINDOW
        totals = []
        for blocks, coarse in units_of(spectra, part):
            powers = [squares(out[:, :LANES], sums[:, :LANES]) for out, sums in blocks]
            for group in members(blocks, coarse):
                kind, t = group[3]
                total = jnp.broadcast_to(powers[kind][t], (8, LANES))
                for p in range(3):
                    kind, t = group[p]
                    total = jnp.where(lane == p, powers[kind][t], total)
                totals.append(jnp.sum(total, axis=0, keepdims=True))
        total = jnp.concatenate(totals, axis=0)
        scale = 1.0 / jnp.sqrt(total * (2.0 / (float(PATCH) ** 4 * gain * gain)) + 1e-05)
        if section == 0:
            scale_ref[start:stop] = scale
            for index, (out, sums) in enumerate(spectra):
                own_ref[block + index, : SLOTS * tiles] = out[: SLOTS * tiles]
                own_ref[block + index, SLOTS * tiles :] = sums
            return
        correlate(section, part, spectra, scale)

    def correlate(d, part, spectra, other_scale):
        start, stop, block = bounds[part]
        row = rows_of((8, LANES))
        lhs, group_rows, sum_at = [], [], []
        at = 0
        for blocks, coarse in units_of(spectra, part):
            products = []
            for index, (out, sums) in enumerate(blocks):
                own = own_ref[block + index]
                own_rows, own_sums = own[: SLOTS * tiles], own[SLOTS * tiles :]
                body = [(own_rows * tile).astype(BF16) for tile in tiles_of(out[: SLOTS * tiles])]
                tail = [own_sums * tile for tile in tiles_of(sums)]
                products.append((body, tail))
            block += len(blocks)
            groups = members(blocks, coarse)
            pieces = []
            for p in range(4):
                body = [
                    jnp.concatenate([x[SLOTS * t : SLOTS * (t + 1)] for x in products[kind][0]], axis=1)
                    for kind, t in (group[p] for group in groups)
                ]
                tail = products[groups[0][p][0]][1]
                if coarse:
                    tail = [jnp.where(row % 2 == p // 2, x, 0.0) for x in tail]
                body.append(jnp.concatenate([x.astype(BF16) for x in tail], axis=1))
                pieces.append(jnp.concatenate(body, axis=0))
            lhs.append(jnp.concatenate(pieces, axis=1))
            for g in range(len(groups)):
                group_rows.append(at + SLOTS * g)
                base = at + SLOTS * len(groups)
                sum_at.append([base + 2 * g, base + 2 * g + 1] if coarse else [base + g])
            at += SLOTS * len(groups) + 8
        rows = jnp.concatenate([matmul(x, inverse_ref[...]) for x in lhs], axis=0)
        stacked = []
        for r in group_rows:
            piece = rows[r : r + SLOTS]
            stacked.append(jnp.concatenate([piece[:, :LANES], piece[:, LANES:]], axis=0))
        high, low = split_value(jnp.concatenate(stacked, axis=1))
        maps = matmul(last_ref[...], jnp.concatenate([high, low, high], axis=0))
        both = scale_ref[start:stop] * other_scale * (1.0 / (float(PATCH) ** 3 * gain**3))
        for g in range(start, stop):
            at = g - start
            scale = both[at : at + 1] * masks[g]
            value = maps[:, LANES * at : LANES * (at + 1)]
            for r in sum_at[at]:
                value = value + rows[r : r + 1, :LANES]
            value = block_transpose(value * scale)
            if g < fine_groups:
                ref, local_g, cols = fine_out_ref, g, fine_cols
            else:
                ref, local_g, cols = coarse_out_ref, g - fine_groups, coarse_cols
            i, j = divmod(4 * local_g, cols)
            for q in range(WINDOW // 4):
                ref[0, d - 1, i, j : j + 4, LANES * q : LANES * (q + 1)] = value[4 * q : 4 * (q + 1)]

    def clear(d):
        for ref in (fine_out_ref, coarse_out_ref):
            ref[0, d - 1] = jnp.zeros(ref.shape[2:], F32)

    own_copy.wait()
    for index in consts_order(const_count)[:2]:
        const_copies[index].wait()
    analyse(0, "inner")
    for index in consts_order(const_count)[2:]:
        const_copies[index].wait()
    for copy in mask_copies:
        copy.wait()
    masks = mask_rows()
    @pl.when(has_near)
    def _():
        for c in range(CHUNKS):
            near_send[c].wait_recv()
            pl.when(odd & (sec >= 1))(far_relay[c].start)
            pl.when(odd)(near_rim_relay[c].start)

    passes = odd & (sec >= 1)

    @pl.when(has_near & below & passes)
    def _():
        for c in range(CHUNKS):
            near_rim_relay[c].wait_recv()
            far_rim_relay[c].start()

    each(below, rim_send, "wait_recv")
    analyse(0, "outer")

    @pl.when(has_near)
    def _():
        each(below & jnp.logical_not(passes), near_rim_relay, "wait_recv")
        analyse(1, "inner")
        analyse(1, "outer")

    @pl.when(has_far)
    def _():
        for c in range(CHUNKS):
            far_relay[c].wait_recv()
            pl.when(odd)(far_rim_across[c].start)

    @pl.when(has_far)
    def _():
        analyse(2, "inner")
        each(below, far_rim_relay, "wait_recv")
        analyse(2, "outer")

    pl.when(jnp.logical_not(has_near))(lambda: clear(1))
    pl.when(jnp.logical_not(has_far))(lambda: clear(2))
    each(sec >= 1, near_send, "wait_send")
    each(strip >= 1, rim_send, "wait_send")
    each(diagonal, diagonal_send, "wait_send")
    each(routed, routed_send, "wait_send")
    each(odd & has_near & (sec >= 1), far_relay, "wait_send")
    each(odd & has_near, near_rim_relay, "wait_send")
    each(odd & has_near & below & (sec >= 1), far_rim_relay, "wait_send")
    each(odd & has_far, far_rim_across, "wait_send")


def deliver(fine_ref, coarse_ref, fine_out_ref, coarse_out_ref, sem):
    copies = [
        pltpu.make_async_copy(source.at[0, d], target.at[0, d], sem.at[index, d])
        for index, (source, target) in enumerate(((fine_ref, fine_out_ref), (coarse_ref, coarse_out_ref)))
        for d in range(2)
    ]
    for copy in copies:
        copy.start()
    for copy in copies:
        copy.wait()


def local(sections, mask_fine, mask_coarse):
    strip_rows, width = sections.shape[1:]
    consts = [jnp.asarray(t) for t in tables(strip_rows)]
    fine_rows, fine_cols = mask_fine.shape[1:]
    coarse_rows, coarse_cols = mask_coarse.shape[1:]
    count = (fine_rows * fine_cols + coarse_rows * coarse_cols) // 4
    blocks = 4 * fine_rows + 2 * coarse_rows
    vmem = pl.BlockSpec(memory_space=pltpu.VMEM)
    anywhere = pl.BlockSpec(memory_space=pl.ANY)
    flat = WINDOW * WINDOW
    shapes = (
        jax.ShapeDtypeStruct((1, 2, fine_rows, fine_cols, flat), F32),
        jax.ShapeDtypeStruct((1, 2, coarse_rows, coarse_cols, flat), F32),
    )
    operands = [pltpu.with_memory_space_constraint(t, pltpu.HBM) for t in (sections, mask_fine, mask_coarse, *consts)]
    maps = pl.pallas_call(
        functools.partial(compute, len(consts)),
        out_shape=shapes,
        in_specs=[anywhere] * (3 + len(consts)),
        out_specs=(vmem, vmem),
        scratch_shapes=[
            pltpu.VMEM((3, strip_rows, width), BF16),
            pltpu.VMEM((3, strip_rows, width), BF16),
            pltpu.VMEM((blocks, SLOTS * (width // LANES) + 8, LANES), F32),
            pltpu.VMEM((count, LANES), F32),
            pltpu.VMEM(mask_fine.shape, mask_fine.dtype),
            pltpu.VMEM(mask_coarse.shape, mask_coarse.dtype),
            *[pltpu.VMEM(c.shape, c.dtype) for c in consts],
            pltpu.SemaphoreType.DMA,
            pltpu.SemaphoreType.DMA((2,)),
            pltpu.SemaphoreType.DMA((len(consts),)),
            pltpu.SemaphoreType.DMA((8, CHUNKS)),
            pltpu.SemaphoreType.DMA((3, CHUNKS)),
            pltpu.SemaphoreType.DMA((3, CHUNKS)),
        ],
        compiler_params=pltpu.CompilerParams(collective_id=0, has_side_effects=True, vmem_limit_bytes=GRANT),
    )(*operands)
    return pl.pallas_call(
        deliver,
        out_shape=shapes,
        in_specs=[vmem, vmem],
        out_specs=(anywhere, anywhere),
        scratch_shapes=[pltpu.SemaphoreType.DMA((2, 2))],
        compiler_params=pltpu.CompilerParams(vmem_limit_bytes=GRANT),
    )(*maps)


def solution(mesh):
    in_specs = (
        P("sec", "strip", "groups"),
        P("sec", "strip", "groups"),
        P("sec", "strip", "groups"),
    )
    out_specs = (P("sec", None, "strip", "groups", None), P("sec", None, "strip", "groups", None))
    return jax.shard_map(local, mesh=mesh, in_specs=in_specs, out_specs=out_specs, check_vma=False)
```

```python
import functools

import jax
import jax.numpy as jnp
import numpy as np
from jax import lax
from jax.experimental import pallas as pl
from jax.experimental.pallas import tpu as pltpu
from jax.sharding import PartitionSpec as P

PATCH = 64
STRIDE = 32
WINDOW = 32
SLOTS = PATCH // 2
CHUNKS = 2
TABLE_SCALE = 1.869
GRANT = 48 * 1024 * 1024
LANES = 128
F32 = jnp.float32
BF16 = jnp.bfloat16
MESH = pl.DeviceIdType.MESH


def trig(phase):
    angle = 2.0 * np.pi / PATCH * np.mod(phase, PATCH)
    return np.round(np.cos(angle), 12), np.round(np.sin(angle), 12)


def split(table):
    high = np.asarray(table, np.float32).astype(BF16)
    low = (np.asarray(table, np.float64) - high.astype(np.float64)).astype(np.float32).astype(BF16)
    return high, low


def block_diagonal(block, count):
    return np.kron(np.eye(count), block)


def rounded(table):
    scaled = np.asarray(table, np.float64) * TABLE_SCALE
    return scaled.astype(np.float32).astype(BF16)


def table_gain():
    c, _ = trig(np.arange(PATCH))
    return float(c @ rounded(c).astype(np.float64) / (c @ c))


def inner_rows(strip_rows):
    return len([i for i in range(strip_rows // STRIDE) if STRIDE * i + PATCH <= strip_rows])


def tables(strip_rows):
    fine_rows = strip_rows // STRIDE
    coarse_rows = strip_rows // (2 * STRIDE)
    inner = inner_rows(strip_rows)
    height = strip_rows + PATCH
    k = np.concatenate([[PATCH // 2], np.arange(1, SLOTS)])[:, None]
    x = np.arange(height)[None, :]
    units, sums = [], []
    for i in range(fine_rows):
        inside = ((x >= STRIDE * i) & (x < STRIDE * i + PATCH)) * 1.0
        c, s = trig(k * (x - STRIDE * i))
        units.append(np.concatenate([c * inside, -s * inside]))
        sums.append(np.repeat(inside, 8, axis=0))
    for i in range(coarse_rows):
        xc = x // 2 - STRIDE * i
        inside = ((xc >= 0) & (xc < PATCH)) * 0.25
        c, s = trig(k * xc)
        units.append(np.concatenate([c * inside, -s * inside]))
        sums.append(np.repeat(inside, 8, axis=0))

    def first(at, rows):
        high, low = split(np.concatenate(units[at] + sums[at], axis=0)[:, :rows])
        return np.concatenate([high, low], axis=1)

    firsts = [first(slice(inner, None), height)]
    if inner:
        firsts.insert(0, first(slice(0, inner), strip_rows))

    lane = np.arange(LANES)
    half, quarter = LANES // 2, LANES // 4
    middle = (lane >= quarter) & (lane < 3 * quarter)
    windows = [
        (lane % half, lane >= half),
        (np.where(middle, lane - quarter, np.where(lane < quarter, lane + quarter, lane - 3 * quarter)), ~middle),
        (lane % half, lane < half),
        (np.where(lane < quarter, lane + quarter, np.where(middle, lane - quarter, lane - 3 * quarter)), middle),
    ]
    freq = np.arange(PATCH)[None, :]

    def weights(y, is_imag):
        c, s = trig(y[:, None] * freq)
        from_real = np.concatenate([c, -s, -s, -c], axis=1)
        from_imag = np.concatenate([s, c, c, -s], axis=1)
        return rounded(np.where(is_imag[:, None], from_imag, from_real))

    fine_w = np.concatenate([np.concatenate([weights(*w)] * 2, axis=0) for w in windows], axis=0)
    both = np.arange(2 * LANES) >= LANES
    coarse_w = np.concatenate(
        [weights(np.concatenate([at // 2] * 2), both) for at in (lane, (lane + half) % LANES)], axis=0
    )

    shift = np.arange(WINDOW) - WINDOW // 2
    c, s = trig((np.arange(LANES) % PATCH)[:, None] * shift[None, :])
    inverse = []
    for p in range(4):
        block = np.zeros((2 * LANES, 2 * LANES))
        block[:LANES, WINDOW * p : WINDOW * (p + 1)] = c
        block[:LANES, LANES + WINDOW * p : LANES + WINDOW * (p + 1)] = s
        block[LANES:, WINDOW * p : WINDOW * (p + 1)] = -s
        block[LANES:, LANES + WINDOW * p : LANES + WINDOW * (p + 1)] = c
        inverse.append(rounded(block))

    weight = np.where(k == PATCH // 2, 1.0, 2.0)
    c, s = trig(shift[:, None] * k.T)
    last_high, last_low = split(np.concatenate([c * weight.T, -s * weight.T], axis=1))
    last = np.concatenate([last_high, last_high, last_low], axis=1)
    return [fine_w, coarse_w, np.concatenate(inverse, axis=0), last, *firsts]


def split_value(value):
    high = value.astype(BF16)
    return high, (value - high.astype(F32)).astype(BF16)


def matmul(a, b):
    return jnp.dot(a, b, preferred_element_type=F32)


def lanes_of(shape):
    return lax.broadcasted_iota(jnp.int32, shape, 1)


def rows_of(shape):
    return lax.broadcasted_iota(jnp.int32, shape, 0)


def tiles_of(value):
    return [value[:, LANES * t : LANES * (t + 1)] for t in range(value.shape[1] // LANES)]


def window(kind, real, turned, real_next, turned_next):
    lane = lanes_of(real.shape)
    half, quarter = LANES // 2, LANES // 4
    if kind == 0:
        return jnp.where(lane < half, real, turned)
    if kind == 1:
        return jnp.where((lane >= quarter) & (lane < 3 * quarter), real, turned)
    if kind == 2:
        return jnp.where(lane < half, turned, real)
    left = jnp.where(lane < quarter, real_next, turned)
    right = jnp.where(lane < 3 * quarter, turned_next, real)
    return jnp.where(lane < half, left, right)


def sum_rows(tiles):
    row = rows_of((8, LANES))
    tiles = [*tiles, jnp.zeros_like(tiles[0])]
    count = len(tiles) - 1

    def spread(parts):
        out = parts[count - 1]
        for t in range(count - 1):
            out = jnp.where(row % count == t, parts[t], out)
        return out

    return spread(tiles[:-1]), spread(tiles[1:])


def sum_parts(value, count):
    first = rows_of(value.shape) < count
    high, rest = split_value(value)
    high = high.astype(F32)
    middle = rest.astype(F32)
    low = value - high - middle
    return jnp.where(first, high, low).astype(BF16), jnp.where(first, middle, 0.0).astype(BF16)


def section_spectra(loads, first, fine_w_ref, coarse_w_ref, fine_rows, coarse_rows, columns):
    units = fine_rows + coarse_rows
    zero = jnp.zeros((SLOTS, LANES), BF16)
    blank = jnp.zeros((8, LANES), F32)
    reals, imags, sum_tiles = ([[] for _ in range(units)] for _ in range(3))
    for load in loads:
        pixels = load()
        rows = matmul(first, jnp.concatenate([pixels, pixels], axis=0))
        for unit in range(units):
            at = 2 * SLOTS * unit
            real, imag = tiles_of(rows[at : at + SLOTS]), tiles_of(rows[at + SLOTS : at + 2 * SLOTS])
            if unit < fine_rows:
                imag = [pltpu.roll(tile, LANES // 2, 1) for tile in imag]
            reals[unit] += [split_value(tile) for tile in real]
            imags[unit] += [split_value(tile) for tile in imag]
            at = 2 * SLOTS * units + 8 * unit
            sum_tiles[unit] += tiles_of(rows[at : at + 8])
    count = len(sum_tiles[0])
    done = []

    def finish(out):
        sums = out[SLOTS * count : SLOTS * count + 8]
        sums = sums + pltpu.roll(sums, 4, 0)
        sums = jnp.where(lanes_of(sums.shape) % PATCH == 0, 0.0, sums)
        done.append((out, sums))

    for unit in range(units):
        real, imag = reals[unit] + [(zero, zero)], imags[unit] + [(zero, zero)]
        now, following = sum_rows(sum_tiles[unit])
        if unit < fine_rows:
            for kind in range(4):
                lhs = [
                    jnp.concatenate(
                        [window(kind, real[t][h], imag[t][h], real[t + 1][h], imag[t + 1][h]) for h in range(2)], axis=1
                    )
                    for t in range(count)
                ]
                sums = sum_parts(window(kind, now, blank, following, blank), count)
                lhs.append(jnp.concatenate(sums, axis=1))
                weights = fine_w_ref[2 * LANES * kind : 2 * LANES * (kind + 1), :columns]
                finish(matmul(jnp.concatenate(lhs, axis=0), weights))
        else:
            lower = lanes_of((SLOTS, LANES)) < LANES // 2
            low_sums = lanes_of((8, LANES)) < LANES // 2
            for kind in range(2):
                sums = sum_parts(jnp.where(low_sums, following, now) if kind else now, count)
                weights = coarse_w_ref[2 * LANES * kind : 2 * LANES * (kind + 1), :columns]
                out = None
                for h in range(2):
                    lhs = [
                        jnp.concatenate(
                            [
                                jnp.where(lower, part[t + 1][h], part[t][h]) if kind else part[t][h]
                                for part in (real, imag)
                            ],
                            axis=1,
                        )
                        for t in range(count)
                    ]
                    lhs.append(jnp.concatenate([sums[h], jnp.zeros_like(sums[h])], axis=1))
                    term = matmul(jnp.concatenate(lhs, axis=0), weights)
                    out = term if out is None else out + term
                finish(out)
    return done


def block_transpose(value):
    row = lax.broadcasted_iota(jnp.int32, value.shape, 0) % 4
    block = lax.broadcasted_iota(jnp.int32, value.shape, 1) // WINDOW
    rows = value.shape[0]
    moved = pltpu.roll(value, 2 * WINDOW, 1)
    other = jnp.where(row < 2, pltpu.roll(moved, rows - 2, 0), pltpu.roll(moved, 2, 0))
    value = jnp.where((row // 2) == (block // 2), value, other)
    right = pltpu.roll(pltpu.roll(value, WINDOW, 1), rows - 1, 0)
    left = pltpu.roll(pltpu.roll(value, LANES - WINDOW, 1), 1, 0)
    other = jnp.where(row % 2 == 0, right, left)
    return jnp.where((row % 2) == (block % 2), value, other)


def consts_order(const_count):
    return (4, 0, *range(5, const_count), 1, 2, 3)


def compute(const_count, *refs):
    pixels_ref, fine_source_ref, coarse_source_ref = refs[:3]
    sources = refs[3 : 3 + const_count]
    fine_out_ref, coarse_out_ref = refs[3 + const_count : 5 + const_count]
    main_ref, rim_ref, own_ref, scale_ref, fine_mask_ref, coarse_mask_ref = refs[5 + const_count : 11 + const_count]
    held = refs[11 + const_count : 11 + 2 * const_count]
    own_sem, mask_sem, const_sem, send_sem, main_sem, rim_sem = refs[11 + 2 * const_count :]
    sec, strip = lax.axis_index("sec"), lax.axis_index("strip")
    secs, strips = lax.axis_size("sec"), lax.axis_size("strip")
    even, odd = strip % 2 == 0, strip % 2 == 1
    below = strip + 1 < strips
    has_near, has_far = sec + 1 < secs, sec + 2 < secs

    barrier = pltpu.get_barrier_semaphore()

    def greet(condition, device):
        @pl.when(condition)
        def _():
            pl.semaphore_signal(barrier, inc=1, device_id=device, device_id_type=MESH)

    greet(has_near, {"sec": sec + 1})
    greet(even & has_far, {"sec": sec + 2})
    greet(odd & has_near & below, {"sec": sec + 1, "strip": strip + 1})
    greet(below, {"strip": strip + 1})

    own_copy = pltpu.make_async_copy(pixels_ref.at[0], main_ref.at[0], own_sem)
    own_copy.start()
    const_copies = [
        pltpu.make_async_copy(source, target, const_sem.at[index])
        for index, (source, target) in enumerate(zip(sources, held))
    ]
    for index in consts_order(const_count):
        const_copies[index].start()
    mask_copies = [
        pltpu.make_async_copy(source, target, mask_sem.at[index])
        for index, (source, target) in enumerate(
            ((fine_source_ref, fine_mask_ref), (coarse_source_ref, coarse_mask_ref))
        )
    ]
    for copy in mask_copies:
        copy.start()

    diagonal = even & (sec >= 1) & (strip >= 1)
    routed = even & (sec >= 2)
    one = lambda condition: jnp.where(condition, 1, 0)
    targets = one(sec >= 1) + one(strip >= 1) + one(diagonal) + one(routed)

    @pl.when(targets >= 1)
    def _():
        pl.semaphore_wait(barrier, targets)

    piece = pixels_ref.shape[2] // CHUNKS

    def remote(flow, source, target, sems, section, device):
        def chunk(c):
            columns = (slice(None), pl.ds(piece * c, piece))
            return pltpu.make_async_remote_copy(
                src_ref=source.at[columns],
                dst_ref=target.at[section].at[columns],
                send_sem=send_sem.at[flow, c],
                recv_sem=sems.at[section, c],
                device_id=device,
                device_id_type=MESH,
            )

        return [chunk(c) for c in range(CHUNKS)]

    own = pixels_ref.at[0]
    above, before = {"strip": strip - 1}, {"sec": sec - 1}
    near_send = remote(0, own, main_ref, main_sem, 1, before)
    rim_send = remote(1, own, rim_ref, rim_sem, 0, above)
    diagonal_send = remote(2, own, rim_ref, rim_sem, 1, {"sec": sec - 1, "strip": strip - 1})
    routed_send = remote(3, own, main_ref, main_sem, 2, {"sec": sec - 2})
    far_relay = remote(4, main_ref.at[1], main_ref, main_sem, 2, before)
    near_rim_relay = remote(5, main_ref.at[1], rim_ref, rim_sem, 1, above)
    far_rim_relay = remote(6, rim_ref.at[1], rim_ref, rim_sem, 2, before)
    far_rim_across = remote(7, main_ref.at[2], rim_ref, rim_sem, 2, above)

    def each(condition, copies, method):
        @pl.when(condition)
        def _():
            for copy in copies:
                getattr(copy, method)()

    each(odd & (sec >= 1), near_send, "start")
    each(strip >= 1, rim_send, "start")
    each(diagonal, diagonal_send, "start")
    each(even & (sec >= 1), near_send, "start")
    each(routed, routed_send, "start")

    @pl.when(jnp.logical_not(below))
    def _():
        rim_ref[...] = jnp.zeros_like(rim_ref)

    fine_rows, fine_cols = fine_mask_ref.shape[1:]
    coarse_rows, coarse_cols = coarse_mask_ref.shape[1:]
    fine_groups = fine_rows * fine_cols // 4
    count = fine_groups + coarse_rows * coarse_cols // 4
    fine_w_ref, coarse_w_ref, inverse_ref, last_ref = held[:4]
    first_refs = held[4:]
    inner = inner_rows(pixels_ref.shape[1])
    tiles = pixels_ref.shape[2] // LANES
    bounds = {
        "inner": (0, inner * tiles, 0),
        "outer": (inner * tiles, count, 4 * inner),
    }
    gain = table_gain()

    def spread(mask, cols):
        source = lax.broadcasted_iota(jnp.int32, (cols, cols * WINDOW), 0)
        target = lax.broadcasted_iota(jnp.int32, (cols, cols * WINDOW), 1) // WINDOW
        picks = jnp.where(source == target, 1.0, 0.0).astype(BF16)
        return matmul(mask.astype(F32).astype(BF16), picks)

    def mask_rows():
        fine_mask = spread(fine_mask_ref[0], fine_cols)
        coarse_mask = spread(coarse_mask_ref[0], coarse_cols)
        return [
            m[r : r + 1, LANES * t : LANES * (t + 1)]
            for m in (fine_mask, coarse_mask)
            for r in range(m.shape[0])
            for t in range(m.shape[1] // LANES)
        ]

    def squares(out, sums):
        row = rows_of((8, LANES))
        extra = sums * sums * 0.5
        parts = []
        for t in range(tiles):
            block = out[SLOTS * t : SLOTS * (t + 1)]
            block = block * block
            total = jnp.where(row == 0, 0.5 * block[:8], block[:8])
            for r in range(8, SLOTS, 8):
                total = total + block[r : r + 8]
            total = total + jnp.where(row == t, extra, 0.0)
            parts.append(jnp.sum(total, axis=1, keepdims=True))
        return parts

    def members(blocks, coarse):
        if not coarse:
            return [[(kind, t) for kind in range(4)] for t in range(tiles)]
        return [[(p % 2, 2 * g + p // 2) for p in range(4)] for g in range(tiles // 2)]

    def units_of(spectra, part):
        number = (inner if part == "inner" else fine_rows - inner) * 4
        found = [(spectra[at : at + 4], False) for at in range(0, number, 4)]
        return found + [(spectra[at : at + 2], True) for at in range(number, len(spectra), 2)]

    def analyse(section, part, waits=()):
        start, stop, block = bounds[part]
        if start == stop:
            return
        rows = (inner, 0) if part == "inner" else (fine_rows - inner, coarse_rows)

        def load(at, wait=None):
            if wait is not None:
                each(below, [wait], "wait_recv")
            main = main_ref[section, :, at]
            return main if part == "inner" else jnp.concatenate([main, rim_ref[section, :, at]], axis=0)

        loads = [functools.partial(load, slice(None))]
        if waits:
            loads = [
                functools.partial(load, slice(piece * c, piece * (c + 1)), wait) for c, wait in enumerate(waits)
            ]
        first = first_refs[0 if part == "inner" else -1][...]
        columns = LANES if section == 0 else 2 * LANES
        spectra = section_spectra(loads, first, fine_w_ref, coarse_w_ref, *rows, columns)
        lane = lanes_of((8, LANES)) // WINDOW
        totals = []
        for blocks, coarse in units_of(spectra, part):
            powers = [squares(out[:, :LANES], sums[:, :LANES]) for out, sums in blocks]
            for group in members(blocks, coarse):
                kind, t = group[3]
                total = jnp.broadcast_to(powers[kind][t], (8, LANES))
                for p in range(3):
                    kind, t = group[p]
                    total = jnp.where(lane == p, powers[kind][t], total)
                totals.append(jnp.sum(total, axis=0, keepdims=True))
        total = jnp.concatenate(totals, axis=0)
        scale = 1.0 / jnp.sqrt(total * (2.0 / (float(PATCH) ** 4 * gain * gain)) + 1e-05)
        if section == 0:
            scale_ref[start:stop] = scale
            for index, (out, sums) in enumerate(spectra):
                own_ref[block + index, : SLOTS * tiles] = out[: SLOTS * tiles]
                own_ref[block + index, SLOTS * tiles :] = sums
            return
        correlate(section, part, spectra, scale)

    def correlate(d, part, spectra, other_scale):
        start, stop, block = bounds[part]
        row = rows_of((8, LANES))
        lhs, group_rows, sum_at = [], [], []
        at = 0
        for blocks, coarse in units_of(spectra, part):
            products = []
            for index, (out, sums) in enumerate(blocks):
                own = own_ref[block + index]
                own_rows, own_sums = own[: SLOTS * tiles], own[SLOTS * tiles :]
                body = [(own_rows * tile).astype(BF16) for tile in tiles_of(out[: SLOTS * tiles])]
                tail = [own_sums * tile for tile in tiles_of(sums)]
                products.append((body, tail))
            block += len(blocks)
            groups = members(blocks, coarse)
            pieces = []
            for p in range(4):
                body = [
                    jnp.concatenate([x[SLOTS * t : SLOTS * (t + 1)] for x in products[kind][0]], axis=1)
                    for kind, t in (group[p] for group in groups)
                ]
                tail = products[groups[0][p][0]][1]
                if coarse:
                    tail = [jnp.where(row % 2 == p // 2, x, 0.0) for x in tail]
                body.append(jnp.concatenate([x.astype(BF16) for x in tail], axis=1))
                pieces.append(jnp.concatenate(body, axis=0))
            lhs.append(jnp.concatenate(pieces, axis=1))
            for g in range(len(groups)):
                group_rows.append(at + SLOTS * g)
                base = at + SLOTS * len(groups)
                sum_at.append([base + 2 * g, base + 2 * g + 1] if coarse else [base + g])
            at += SLOTS * len(groups) + 8
        rows = jnp.concatenate([matmul(x, inverse_ref[...]) for x in lhs], axis=0)
        stacked = []
        for r in group_rows:
            piece = rows[r : r + SLOTS]
            stacked.append(jnp.concatenate([piece[:, :LANES], piece[:, LANES:]], axis=0))
        high, low = split_value(jnp.concatenate(stacked, axis=1))
        maps = matmul(last_ref[...], jnp.concatenate([high, low, high], axis=0))
        both = scale_ref[start:stop] * other_scale * (1.0 / (float(PATCH) ** 3 * gain**3))
        for g in range(start, stop):
            at = g - start
            scale = both[at : at + 1] * masks[g]
            value = maps[:, LANES * at : LANES * (at + 1)]
            for r in sum_at[at]:
                value = value + rows[r : r + 1, :LANES]
            value = block_transpose(value * scale)
            if g < fine_groups:
                ref, local_g, cols = fine_out_ref, g, fine_cols
            else:
                ref, local_g, cols = coarse_out_ref, g - fine_groups, coarse_cols
            i, j = divmod(4 * local_g, cols)
            for q in range(WINDOW // 4):
                ref[0, d - 1, i, j : j + 4, LANES * q : LANES * (q + 1)] = value[4 * q : 4 * (q + 1)]

    def clear(d):
        for ref in (fine_out_ref, coarse_out_ref):
            ref[0, d - 1] = jnp.zeros(ref.shape[2:], F32)

    own_copy.wait()
    for index in consts_order(const_count)[:2]:
        const_copies[index].wait()
    analyse(0, "inner")
    for index in consts_order(const_count)[2:]:
        const_copies[index].wait()
    for copy in mask_copies:
        copy.wait()
    masks = mask_rows()
    @pl.when(has_near)
    def _():
        for c in range(CHUNKS):
            near_send[c].wait_recv()
            pl.when(odd & (sec >= 1))(far_relay[c].start)
            pl.when(odd)(near_rim_relay[c].start)

    passes = odd & (sec >= 1)

    @pl.when(has_near & below & passes)
    def _():
        for c in range(CHUNKS):
            near_rim_relay[c].wait_recv()
            far_rim_relay[c].start()

    each(below, rim_send, "wait_recv")
    analyse(0, "outer")

    @pl.when(has_near)
    def _():
        each(below & jnp.logical_not(passes), near_rim_relay, "wait_recv")
        analyse(1, "inner")
        analyse(1, "outer")

    @pl.when(has_far)
    def _():
        for c in range(CHUNKS):
            far_relay[c].wait_recv()
            pl.when(odd)(far_rim_across[c].start)

    pl.when(jnp.logical_not(has_near))(lambda: clear(1))
    pl.when(jnp.logical_not(has_far))(lambda: clear(2))

    @pl.when(has_far)
    def _():
        analyse(2, "inner")

    each(sec >= 1, near_send, "wait_send")
    each(strip >= 1, rim_send, "wait_send")
    each(diagonal, diagonal_send, "wait_send")
    each(routed, routed_send, "wait_send")
    each(odd & has_near & (sec >= 1), far_relay, "wait_send")
    each(odd & has_near, near_rim_relay, "wait_send")
    each(odd & has_near & below & (sec >= 1), far_rim_relay, "wait_send")

    @pl.when(has_far)
    def _():
        each(below, far_rim_relay, "wait_recv")
        analyse(2, "outer")

    each(odd & has_far, far_rim_across, "wait_send")


def deliver(fine_ref, coarse_ref, fine_out_ref, coarse_out_ref, sem):
    copies = [
        pltpu.make_async_copy(source.at[0, d], target.at[0, d], sem.at[index, d])
        for index, (source, target) in enumerate(((fine_ref, fine_out_ref), (coarse_ref, coarse_out_ref)))
        for d in range(2)
    ]
    for copy in copies:
        copy.start()
    for copy in copies:
        copy.wait()


def local(sections, mask_fine, mask_coarse):
    strip_rows, width = sections.shape[1:]
    consts = [jnp.asarray(t) for t in tables(strip_rows)]
    fine_rows, fine_cols = mask_fine.shape[1:]
    coarse_rows, coarse_cols = mask_coarse.shape[1:]
    count = (fine_rows * fine_cols + coarse_rows * coarse_cols) // 4
    blocks = 4 * fine_rows + 2 * coarse_rows
    vmem = pl.BlockSpec(memory_space=pltpu.VMEM)
    anywhere = pl.BlockSpec(memory_space=pl.ANY)
    flat = WINDOW * WINDOW
    shapes = (
        jax.ShapeDtypeStruct((1, 2, fine_rows, fine_cols, flat), F32),
        jax.ShapeDtypeStruct((1, 2, coarse_rows, coarse_cols, flat), F32),
    )
    operands = [pltpu.with_memory_space_constraint(t, pltpu.HBM) for t in (sections, mask_fine, mask_coarse, *consts)]
    maps = pl.pallas_call(
        functools.partial(compute, len(consts)),
        out_shape=shapes,
        in_specs=[anywhere] * (3 + len(consts)),
        out_specs=(vmem, vmem),
        scratch_shapes=[
            pltpu.VMEM((3, strip_rows, width), BF16),
            pltpu.VMEM((3, strip_rows, width), BF16),
            pltpu.VMEM((blocks, SLOTS * (width // LANES) + 8, LANES), F32),
            pltpu.VMEM((count, LANES), F32),
            pltpu.VMEM(mask_fine.shape, mask_fine.dtype),
            pltpu.VMEM(mask_coarse.shape, mask_coarse.dtype),
            *[pltpu.VMEM(c.shape, c.dtype) for c in consts],
            pltpu.SemaphoreType.DMA,
            pltpu.SemaphoreType.DMA((2,)),
            pltpu.SemaphoreType.DMA((len(consts),)),
            pltpu.SemaphoreType.DMA((8, CHUNKS)),
            pltpu.SemaphoreType.DMA((3, CHUNKS)),
            pltpu.SemaphoreType.DMA((3, CHUNKS)),
        ],
        compiler_params=pltpu.CompilerParams(collective_id=0, has_side_effects=True, vmem_limit_bytes=GRANT),
    )(*operands)
    return pl.pallas_call(
        deliver,
        out_shape=shapes,
        in_specs=[vmem, vmem],
        out_specs=(anywhere, anywhere),
        scratch_shapes=[pltpu.SemaphoreType.DMA((2, 2))],
        compiler_params=pltpu.CompilerParams(vmem_limit_bytes=GRANT),
    )(*maps)


def solution(mesh):
    in_specs = (
        P("sec", "strip", "groups"),
        P("sec", "strip", "groups"),
        P("sec", "strip", "groups"),
    )
    out_specs = (P("sec", None, "strip", "groups", None), P("sec", None, "strip", "groups", None))
    return jax.shard_map(local, mesh=mesh, in_specs=in_specs, out_specs=out_specs, check_vma=False)
```
